128 devices in a mesh: req: 8 (over x, core), mlp: 16 (over y, z).
Axes of the slice: x: 4, y: 4, z: 4, core: 2. Of those that a mesh axis runs over, the one named last changes fastest.
Arguments:
- queries: bfloat16 [4096, 4096], P(('req', 'mlp')), may hold values from -80 to 80
- keys: bfloat16 [4096, 4096], P(('req', 'mlp')), may hold values from -4 to 4
- values: bfloat16 [4096, 4096], P(('req', 'mlp')), may hold values from -6 to 6
- block_hidden_input: bfloat16 [4096, 5120], P(('req', 'mlp')), may hold values from -6 to 6
- attention_out_weight: bfloat16 [4096, 5120], P('mlp'), may hold values from -0.09375 to 0.09375
- feedfwd_in_weight: bfloat16 [5120, 13824], P(None, 'mlp'), may hold values from -0.078125 to 0.078125
- feedfwd_out_weight: bfloat16 [13824, 5120], P('mlp'), may hold values from -0.0546875 to 0.0546875
- norm_gain_vector: float32 [5120], replicated, may hold values from 0.5 to 1.5
- norm_bias_vector: float32 [5120], replicated, may hold values from -3 to 3
- adapter_down_factors: bfloat16 [64, 5120, 16], P('req', 'mlp'), may hold values from -0.078125 to 0.078125
- adapter_up_factors: bfloat16 [64, 16, 13824], P('req', None, 'mlp'), may hold values from -0.75 to 0.75
- paged_key_cache: bfloat16 [40, 128, 4096], P('req', None, 'mlp'), may hold values from -6 to 6
- paged_value_cache: bfloat16 [40, 128, 4096], P('req', None, 'mlp'), may hold values from -6 to 6
- request_prompt_length: int32 [8, 16], P('req'), may hold values from 1 to 256, 512 in all within a row
- group_page_lookup: int32 [8, 4], P('req'), may hold values from 0 to 4, as said below
- adapter_per_request: int32 [8, 16], P('req'), may hold values from 0 to 63
- adapter_bank_slot: int32 [64], replicated, may hold values from 0 to 63, each once
Outputs:
- block_out: bfloat16 [4096, 5120], P(('req', 'mlp'))
- key_pages_out: bfloat16 [40, 128, 4096], P('req', None, 'mlp')
- value_pages_out: bfloat16 [40, 128, 4096], P('req', None, 'mlp')
The draws below stay inside these ranges and needn't reach their ends.
Inputs may be any that keep to these rules, and one draw needn't show every extreme that they name: `group_page_lookup`: the 4 entries of a row are different pages of the group's 5. `request_prompt_length`: each row sums to 512; its longest request holds exactly half of that.
All inputs are finite; a program needn't handle non-finite values.
Results may differ from the reference program's by a relative error of at most 0.014.
Values may be sent and summed in bfloat16 or wider, within the bound.
A program may use at most 128 MiB of HBM per device.

```python
import math
import jax
import jax.numpy as jnp
import numpy as np
from jax import lax

MODEL_WIDTH = 5120
HEADS = 32
HS = 128
FEEDFWD_UNITS = 13824
ADAPTER_RANK = 16
ADAPTER_COUNT = 64
REQS = 16
PAGE = 128
TOK_DEV = 32
TOK_G = 512
TOKENS = 4096
BLOCKS = 4
PAGES = 5
N_REQ = 8
N_MLP = 16


def drawn_pair(key):
    head_width = HEADS * HS
    queries = jnp.clip(jax.random.normal(jax.random.fold_in(key, 11), (TOKENS, head_width), jnp.float32), -4.0, 4.0)
    keys = jnp.clip(jax.random.normal(jax.random.fold_in(key, 12), (TOKENS, head_width), jnp.float32), -4.0, 4.0)
    return (queries, keys)


def draw_queries(key, part):
    return drawn_pair(key)[0].astype(jnp.bfloat16)


def draw_keys(key, part):
    return drawn_pair(key)[1].astype(jnp.bfloat16)


def draw_group_page_lookup(key, part):

    def one_group(group_number):
        chosen = jax.random.permutation(jax.random.fold_in(key, group_number), PAGES)[:BLOCKS]
        holds_last = jnp.any(chosen == PAGES - 1)
        return chosen.at[0].set(jnp.where(holds_last, chosen[0], PAGES - 1))
    return jax.vmap(one_group)(jnp.arange(N_REQ)).astype(jnp.int32)


def place_ends(entries, rng, low, high):
    longest = entries.shape.index(max(entries.shape))
    spots = []
    for shift in (0, 1):
        where = [jax.random.randint(jax.random.fold_in(rng, axis), (), 0, length) for axis, length in enumerate(entries.shape)]
        where[longest] = (where[longest] + shift) % entries.shape[longest]
        spots.append(tuple(where))
    return entries.at[spots[0]].set(low).at[spots[1]].set(high)


def block_levels(own_key, dims, cuts, smallest, largest):
    factor_of, own = 1.0, jax.random.fold_in(own_key, 6)
    for dim, blocks in cuts:
        heights = jnp.exp(jax.random.uniform(jax.random.fold_in(own, dim), (blocks,), jnp.float32, smallest / len(cuts), largest / len(cuts)))
        factor_of = factor_of * jnp.repeat(heights, dims[dim] // blocks).reshape([-1 if axis == dim else 1 for axis in range(len(dims))])
    return factor_of


def rank_table(number_of, skew):
    loads = [(1 << 20) // math.isqrt(rank ** skew) + 1 for rank in range(1, number_of + 1)]
    scale = 1 + sum(loads) // (1 << 30)
    return np.cumsum(np.array([max(1, weight // scale) for weight in loads]))


def ranked_ids(rng, extent, number_of, lean):
    grid = rank_table(number_of, lean)
    ticket = jax.random.randint(jax.random.fold_in(rng, 1), extent, 0, int(grid[number_of - 1]))
    rank = jnp.searchsorted(jnp.asarray(grid, jnp.int32), ticket, side="right")
    return jax.random.permutation(jax.random.fold_in(rng, 2), number_of)[rank].astype(jnp.int32)


def length_profile(count, total, reach, skew):
    portions = [(1 << 20) // math.isqrt(rank ** skew) + 1 for rank in range(2, count + 1)]
    spare, counts = total - reach - (count - 1), [1] * (count - 1)
    while spare > 0:
        free = [i for i in range(count - 1) if counts[i] < reach]
        pool, left = sum([portions[i] for i in free]), spare
        for i in free:
            more = min(reach - counts[i], max(1, left * portions[i] // pool), spare)
            counts[i] = counts[i] + more
            spare = spare - more
    return np.array([reach] + counts)


def ragged(stream_key, count, total, bound, skew):
    if count == 2:
        one = jax.random.randint(stream_key, (), max(1, total - bound), min(bound, total - 1) + 1)
        return jnp.stack([one, total - one])
    sizes = jnp.asarray(length_profile(count, total, bound, skew), jnp.int32)
    twos = (count - 1) // 2
    source_of, sink = sizes[1:1 + 2 * twos:2], sizes[2:2 + 2 * twos:2]
    room = jnp.minimum(source_of - 1, bound - sink)
    passed = jax.random.randint(jax.random.fold_in(stream_key, 1), (twos,), 0, 1 << 20) % (room + 1)
    sizes = sizes.at[1:1 + 2 * twos:2].set(source_of - passed).at[2:2 + 2 * twos:2].set(sink + passed)
    return sizes[jax.random.permutation(jax.random.fold_in(stream_key, 2), count)]


def bell_draw(key, dims, deviation, bound, shards=(), held_as=jnp.bfloat16):
    factor_of = block_levels(key, dims, shards, -0.22, 0.18) if shards else 1.0
    values = jax.random.normal(key, dims, jnp.float32) * deviation * factor_of
    return jnp.minimum(jnp.maximum(values, -bound), bound).astype(held_as)


def setup_inputs(seed: int = 0) -> dict:
    seeds = jax.random.split(jax.random.key(seed), 18)
    queries = draw_queries(jax.random.fold_in(seeds[17], 71), 0)
    keys = draw_keys(jax.random.fold_in(seeds[17], 71), 0)
    values = bell_draw(seeds[2], (TOKENS, HEADS * HS), 1.0, 6.0, ((0, 128),))
    block_hidden_input = bell_draw(seeds[3], (TOKENS, MODEL_WIDTH), 1.0, 6.0, ((0, 128),))
    attention_out_weight = bell_draw(seeds[4], (HEADS * HS, MODEL_WIDTH), (HEADS * HS) ** -0.5, 0.09375, ((0, 16),))
    feedfwd_in_weight = bell_draw(seeds[5], (MODEL_WIDTH, FEEDFWD_UNITS), MODEL_WIDTH ** -0.5, 0.078125, ((1, 16),))
    feedfwd_out_weight = bell_draw(seeds[6], (FEEDFWD_UNITS, MODEL_WIDTH), FEEDFWD_UNITS ** -0.5, 0.0546875, ((0, 16),))
    norm_gain_vector = jnp.clip(1.0 + 0.1 * jax.random.normal(seeds[7], (MODEL_WIDTH,), jnp.float32), 0.5, 1.5)
    norm_bias_vector = bell_draw(seeds[8], (MODEL_WIDTH,), 0.5, 3.0, (), jnp.float32)
    adapter_down_factors = bell_draw(seeds[9], (ADAPTER_COUNT, MODEL_WIDTH, ADAPTER_RANK), MODEL_WIDTH ** -0.5, 0.078125, ((0, 8), (1, 16)))
    adapter_up_factors = bell_draw(seeds[10], (ADAPTER_COUNT, ADAPTER_RANK, FEEDFWD_UNITS), (4 * ADAPTER_RANK) ** -0.5, 0.75, ((0, 8), (2, 16)))
    paged_key_cache = bell_draw(seeds[11], (N_REQ * PAGES, PAGE, HEADS * HS), 1.0, 6.0, ((0, 8), (2, 16)))
    paged_value_cache = bell_draw(seeds[12], (N_REQ * PAGES, PAGE, HEADS * HS), 1.0, 6.0, ((0, 8), (2, 16)))
    request_prompt_length = jax.vmap(lambda own: ragged(own, REQS, TOK_G, TOK_G // 2, 2))(jax.random.split(seeds[13], N_REQ)).reshape((N_REQ, REQS)).astype(jnp.int32)
    group_page_lookup = draw_group_page_lookup(jax.random.fold_in(seeds[17], 71), 0)
    adapter_per_request = place_ends(ranked_ids(seeds[15], (N_REQ, REQS), ADAPTER_COUNT, 2), jax.random.fold_in(seeds[15], 3), 0, ADAPTER_COUNT - 1).astype(jnp.int32)
    adapter_bank_slot = jax.random.permutation(seeds[16], ADAPTER_COUNT).astype(jnp.int32)
    return {"queries": queries, "keys": keys, "values": values, "block_hidden_input": block_hidden_input, "attention_out_weight": attention_out_weight, "feedfwd_in_weight": feedfwd_in_weight, "feedfwd_out_weight": feedfwd_out_weight, "norm_gain_vector": norm_gain_vector, "norm_bias_vector": norm_bias_vector, "adapter_down_factors": adapter_down_factors, "adapter_up_factors": adapter_up_factors, "paged_key_cache": paged_key_cache, "paged_value_cache": paged_value_cache, "request_prompt_length": request_prompt_length, "group_page_lookup": group_page_lookup, "adapter_per_request": adapter_per_request, "adapter_bank_slot": adapter_bank_slot}


EPS = 1e-06

def modulate(residual, norm_gain_vector, norm_bias_vector):
    row_mean = lax.optimization_barrier(jnp.mean(residual, axis=-1, keepdims=True))
    centered = residual - row_mean
    row_var = lax.optimization_barrier(jnp.mean(centered * centered, axis=-1, keepdims=True))
    return (centered * lax.rsqrt(row_var + EPS) * norm_gain_vector + norm_bias_vector).astype(jnp.bfloat16)

def softmax_rows(scores, allowed):
    masked = jnp.where(allowed, scores, -1e+30)
    row_peak = lax.optimization_barrier(jnp.max(masked, axis=-1, keepdims=True))
    exponent = jnp.exp(masked - row_peak)
    return (exponent / lax.optimization_barrier(jnp.sum(exponent, axis=-1, keepdims=True))).astype(jnp.bfloat16)

def block_rounded_product(left, right, blocks):
    inner = left.shape[1] // blocks
    result = jnp.zeros((left.shape[0], right.shape[1]), jnp.float32)
    for index_block in range(blocks):
        block_sum = jnp.dot(left[:, index_block * inner:(index_block + 1) * inner], right[index_block * inner:(index_block + 1) * inner], preferred_element_type=jnp.float32)
        rounded = lax.optimization_barrier(block_sum.astype(jnp.bfloat16))
        result = result + rounded.astype(jnp.float32)
    return result

def reference(queries, keys, values, block_hidden_input, attention_out_weight, feedfwd_in_weight, feedfwd_out_weight, norm_gain_vector, norm_bias_vector, adapter_down_factors, adapter_up_factors, paged_key_cache, paged_value_cache, request_prompt_length, group_page_lookup, adapter_per_request, adapter_bank_slot):
    group_rows = TOK_DEV * N_MLP
    head_width = HEADS * HS
    positions = jnp.arange(group_rows, dtype=jnp.int32)
    request_ends = jnp.cumsum(request_prompt_length, axis=1).astype(jnp.int32)
    segments = lax.optimization_barrier(jnp.sum((positions[None, :, None] >= request_ends[:, None, :]).astype(jnp.int32), axis=2)).astype(jnp.int32)
    score_scale = HS ** (-0.5)

    def attend(group_data):
        query_group, key_group, value_group, group_segment = group_data
        query_heads = query_group.reshape(group_rows, HEADS, HS).astype(jnp.float32)
        key_heads = key_group.reshape(group_rows, HEADS, HS).astype(jnp.float32)
        value_heads = value_group.reshape(group_rows, HEADS, HS).astype(jnp.float32)
        scores = jnp.einsum('qhd,khd->hqk', query_heads, key_heads) * score_scale
        allowed = (group_segment[:, None] == group_segment[None, :]) & (positions[None, :] <= positions[:, None])
        weights = softmax_rows(scores, allowed[None]).astype(jnp.float32)
        mixed = jnp.einsum('hqk,khd->qhd', weights, value_heads)
        return mixed.astype(jnp.bfloat16).reshape(group_rows, head_width)
    attended = lax.map(attend, (queries.reshape(N_REQ, group_rows, head_width), keys.reshape(N_REQ, group_rows, head_width), values.reshape(N_REQ, group_rows, head_width), segments)).reshape(TOKENS, head_width)
    group_index = jnp.arange(N_REQ, dtype=jnp.int32)[:, None]
    key_pages_out = paged_key_cache.reshape(N_REQ, PAGES, PAGE, head_width).at[group_index, group_page_lookup].set(keys.reshape(N_REQ, BLOCKS, PAGE, head_width)).reshape(N_REQ * PAGES, PAGE, head_width)
    value_pages_out = paged_value_cache.reshape(N_REQ, PAGES, PAGE, head_width).at[group_index, group_page_lookup].set(values.reshape(N_REQ, BLOCKS, PAGE, head_width)).reshape(N_REQ * PAGES, PAGE, head_width)
    residual = block_hidden_input.astype(jnp.float32) + block_rounded_product(attended, attention_out_weight, N_MLP)
    normed = modulate(residual, norm_gain_vector, norm_bias_vector)
    slots = adapter_bank_slot[adapter_per_request]

    def adapt(group_data):
        normed_group, group_segment, group_bank_slots = group_data
        down_factor_chosen = adapter_down_factors[group_bank_slots].astype(jnp.float32)
        up_factor_chosen = adapter_up_factors[group_bank_slots].astype(jnp.float32)
        chosen = (group_segment[:, None] == jnp.arange(REQS, dtype=jnp.int32)[None, :]).astype(jnp.float32)
        every_rank = jnp.einsum('td,rdk->trk', normed_group.astype(jnp.float32), down_factor_chosen)
        lowrank = lax.optimization_barrier(lax.optimization_barrier(jnp.sum(every_rank * chosen[:, :, None], axis=1)).astype(jnp.bfloat16))
        spread = chosen[:, :, None] * lowrank.astype(jnp.float32)[:, None, :]
        preact = jnp.dot(normed_group, feedfwd_in_weight, preferred_element_type=jnp.float32) + jnp.einsum('trk,rkf->tf', spread, up_factor_chosen)
        return jax.nn.gelu(preact, approximate=True).astype(jnp.bfloat16)
    activated = lax.map(adapt, (normed.reshape(N_REQ, group_rows, MODEL_WIDTH), segments, slots)).reshape(TOKENS, FEEDFWD_UNITS)
    mlp_out = block_rounded_product(activated, feedfwd_out_weight, N_MLP)
    block_out = (residual + mlp_out).astype(jnp.bfloat16)
    return (block_out, key_pages_out, value_pages_out)
```

```python
import functools

import jax
import jax.numpy as jnp
from jax import lax
from jax.experimental import pallas as pl
from jax.experimental.pallas import tpu as pltpu
from jax.sharding import PartitionSpec as P

MESH = pl.DeviceIdType.MESH
HS = 128
RANK = 16
REQS = 16
TOK_G = 512
WIDTH = 5120
HALF = WIDTH // 2
QUART = HALF // 2
UNITS = 864
HEADC = 256
TILE = 512
EPS = 1e-06
F32 = jnp.float32
BF16 = jnp.bfloat16

RELAY_F, RELAY_B, DIR_F, DIR_B, SUM_F, SUM_B = range(6)
R2F, R2B, F2F, F2B = range(24, 28)


def nt_dot(a, b):
    return lax.dot_general(a, b, (((1,), (1,)), ((), ())), preferred_element_type=F32)


def kernel(
    q_hbm, k_hbm, v_hbm, hid_hbm, wo_hbm, wi_hbm, w2_hbm, gain_hbm, bias_hbm, down_hbm, up_hbm, kc_hbm, vc_hbm,
    lens, look, adp, slot,
    out_hbm, ko_hbm, vo_hbm,
    qkv, att, wo, wi, w2, hid, gain, bias, downs, ups, kc, vc, start_col,
    part, norm, relay_f, relay_b, full_f, full_b, mid, relay2_f, relay2_b, full2_f, full2_b,
    resid, total, acc, act, onehot, dsel_f, dsel, usel, low, spread, outb,
    local_sem, a2a_send, a2a_recv, fac_send, fac_recv, low_send, low_recv, rs_send, rs_recv, ag_send, ag_recv,
):
    m = lax.axis_index("mlp")
    r = lax.axis_index("req")
    y, z = lax.div(m, 4), lax.rem(m, 4)

    def place(h, p, s):
        return (p, s) if h == 0 else (s, p)

    def device(h, p, s):
        a, b = place(h, p, s)
        return {"mlp": a * 4 + b}

    prim = (y, z)
    sec = (z, y)

    def up1(i, by):
        return lax.rem(i + by, 4)

    locals_ = {}

    def local(i, src, dst):
        c = pltpu.make_async_copy(src, dst, local_sem.at[i])
        c.start()
        locals_[i] = c

    local(0, wo_hbm, wo)
    local(3, hid_hbm, hid)
    local(4, gain_hbm, gain)
    local(5, bias_hbm, bias)
    local(6, kc_hbm, kc)
    local(7, vc_hbm, vc)
    local(8, down_hbm, downs.at[r])
    local(9, up_hbm, ups.at[r])
    for t, ref in enumerate((q_hbm, k_hbm, v_hbm)):
        cols = pl.ds(pl.multiple_of(m * HEADC, HEADC), HEADC)
        rows = pl.ds(pl.multiple_of(m * 32, 32), 32)
        local(10 + t, ref.at[:, cols], qkv.at[t, rows, :])

    barrier = pltpu.get_barrier_semaphore()

    def greet_mlp(i, c):
        pl.semaphore_signal(barrier, inc=1, device_id={"mlp": lax.rem(m + i, 16)}, device_id_type=MESH)
        return c

    def greet_req(i, c):
        pl.semaphore_signal(barrier, inc=1, device_id={"req": lax.rem(r + i, 8)}, device_id_type=MESH)
        return c

    lax.fori_loop(1, 16, greet_mlp, 0)
    lax.fori_loop(1, 8, greet_req, 0)
    pl.semaphore_wait(barrier, 22)

    def a2a_copy(t, ref, i):
        d = lax.rem(m + i, 16)
        return pltpu.make_async_remote_copy(
            src_ref=ref.at[:, pl.ds(pl.multiple_of(d * HEADC, HEADC), HEADC)],
            dst_ref=qkv.at[t, pl.ds(pl.multiple_of(m * 32, 32), 32), :],
            send_sem=a2a_send.at[t, i],
            recv_sem=a2a_recv.at[t, i],
            device_id={"mlp": d},
            device_id_type=MESH,
        )

    def a2a_start(i, c):
        for t, ref in enumerate((q_hbm, k_hbm, v_hbm)):
            a2a_copy(t, ref, i).start()
        return c

    lax.fori_loop(1, 16, a2a_start, 0)

    def fac_copy(t, src, dst, i):
        return pltpu.make_async_remote_copy(
            src_ref=src,
            dst_ref=dst.at[r],
            send_sem=fac_send.at[t, i],
            recv_sem=fac_recv.at[t, i],
            device_id={"req": lax.rem(r + i, 8)},
            device_id_type=MESH,
        )

    def fac_start(i, c):
        fac_copy(0, down_hbm, downs, i).start()
        fac_copy(1, up_hbm, ups, i).start()
        return c

    lax.fori_loop(1, 8, fac_start, 0)
    local(1, wi_hbm, wi)
    local(2, w2_hbm, w2)

    pos = lax.broadcasted_iota(jnp.int32, (TOK_G, 1), 0)
    starts, ends = [], []
    first = jnp.zeros((TOK_G, 1), jnp.int32)
    end = jnp.int32(0)
    for i in range(REQS):
        starts.append(end)
        end = end + lens[0, i]
        ends.append(end)
        first = jnp.where(pos >= end, end, first)
    start_col[...] = first

    for i in range(REQS):
        wanted = slot[adp[0, i]] * RANK
        lane = lax.broadcasted_iota(jnp.int32, (RANK, 64 * RANK), 1)
        sub = lax.broadcasted_iota(jnp.int32, (RANK, 64 * RANK), 0)
        onehot[i * RANK : (i + 1) * RANK, :] = (lane - sub == wanted).astype(F32).astype(BF16)
    acc[...] = jnp.zeros_like(acc)

    for t in range(3):
        locals_[10 + t].wait()

    def a2a_wait(i, c):
        for t, ref in enumerate((q_hbm, k_hbm, v_hbm)):
            a2a_copy(t, ref, i).wait_recv()
        return c

    lax.fori_loop(1, 16, a2a_wait, 0)

    for h in range(2):
        hc = slice(h * HS, (h + 1) * HS)
        for i in range(4):
            rows, length = slice(i * 128, (i + 1) * 128), (i + 1) * 128
            score = nt_dot(qkv[0, rows, hc], qkv[1, :length, hc]) * (HS ** (-0.5))
            qi = lax.broadcasted_iota(jnp.int32, (128, length), 0) + i * 128
            kj = lax.broadcasted_iota(jnp.int32, (128, length), 1)
            allowed = (kj <= qi) & (kj >= start_col[rows, :])
            score = jnp.where(allowed, score, -1e30)
            expo = jnp.exp(score - jnp.max(score, axis=1, keepdims=True))
            weights = (expo / jnp.sum(expo, axis=1, keepdims=True)).astype(BF16)
            mixed = jnp.dot(weights, qkv[2, :length, hc], preferred_element_type=F32)
            att[i, :, :, hc] = mixed.astype(BF16).reshape(4, 32, HS)

    def remote(src, dst, sems, h, i, dev):
        c = pltpu.make_async_remote_copy(
            src_ref=src,
            dst_ref=dst,
            send_sem=sems[0].at[h, i],
            recv_sem=sems[1].at[h, i],
            device_id=dev,
            device_id_type=MESH,
        )
        c.start()
        return c

    def cols_of(h, which):
        base = h * HALF
        if which == "F":
            return slice(base, base + QUART)
        if which == "B":
            return slice(base + QUART, base + HALF)
        return slice(base, base + HALF)

    def reduce_scatter(left, right, own, fill):
        flying = {}
        sems = (rs_send, rs_recv)

        def view(h, p, s, which):
            a, b = place(h, p, s)
            return part.at[a, b, :, cols_of(h, which)]

        def load(h, p, s, which):
            a, b = place(h, p, s)
            return part[a, b, :, cols_of(h, which)].astype(F32)

        def store(h, p, s, which, value):
            a, b = place(h, p, s)
            part[a, b, :, cols_of(h, which)] = value.astype(BF16)

        def order(h, k):
            return up1(sec[h], (2, 1, 3, 0)[k])

        def product(h, k):
            s = order(h, k)
            lhs = left[:, s] if h == 0 else left[s]
            lhs = lhs.reshape(128, left.shape[3])
            for c in range(h * HALF, (h + 1) * HALF, TILE):
                value = jnp.dot(lhs, right[:, c : c + TILE], preferred_element_type=F32).astype(BF16)
                value = value.reshape(4, 32, TILE)
                if h == 0:
                    part[:, s, :, c : c + TILE] = value
                else:
                    part[s, :, :, c : c + TILE] = value

        def first_sends(h, k):
            p, s, sp = prim[h], sec[h], order(h, k)
            ahead, behind = device(h, up1(p, 1), s), device(h, up1(p, 3), s)
            i = 6 * k
            far = up1(p, 2)
            flying[h, i + RELAY_F] = remote(view(h, far, sp, "F"), relay_f.at[h, k], sems, h, i + RELAY_F, ahead)
            flying[h, i + RELAY_B] = remote(view(h, far, sp, "B"), relay_b.at[h, k], sems, h, i + RELAY_B, behind)
            flying[h, i + DIR_F] = remote(
                view(h, up1(p, 1), sp, "B"), full_f.at[h, k, :, QUART:], sems, h, i + DIR_F, ahead
            )
            flying[h, i + DIR_B] = remote(
                view(h, up1(p, 3), sp, "F"), full_b.at[h, k, :, :QUART], sems, h, i + DIR_B, behind
            )

        def second_sends(h, k):
            p, s, sp = prim[h], sec[h], order(h, k)
            ahead, behind = device(h, up1(p, 1), s), device(h, up1(p, 3), s)
            i = 6 * k
            flying[h, i + RELAY_F].wait_recv()
            store(h, up1(p, 1), sp, "F", load(h, up1(p, 1), sp, "F") + relay_f[h, k].astype(F32))
            flying[h, i + SUM_F] = remote(
                view(h, up1(p, 1), sp, "F"), full_f.at[h, k, :, :QUART], sems, h, i + SUM_F, ahead
            )
            flying[h, i + RELAY_B].wait_recv()
            store(h, up1(p, 3), sp, "B", load(h, up1(p, 3), sp, "B") + relay_b[h, k].astype(F32))
            flying[h, i + SUM_B] = remote(
                view(h, up1(p, 3), sp, "B"), full_b.at[h, k, :, QUART:], sems, h, i + SUM_B, behind
            )

        def third_sends(h, k):
            p, s, sp = prim[h], sec[h], order(h, k)
            for name in (DIR_F, SUM_F, DIR_B, SUM_B):
                flying[h, 6 * k + name].wait_recv()
            value = load(h, p, sp, "W") + full_f[h, k].astype(F32) + full_b[h, k].astype(F32)
            ahead, behind = device(h, p, up1(s, 1)), device(h, p, up1(s, 3))
            if k == 0:
                mid[h, 0] = value.astype(BF16)
                flying[h, R2F] = remote(mid.at[h, 0, :, :QUART], relay2_f.at[h], sems, h, R2F, ahead)
                flying[h, R2B] = remote(mid.at[h, 0, :, QUART:], relay2_b.at[h], sems, h, R2B, behind)
            elif k == 1:
                flying[h, R2F].wait_recv()
                mid[h, 1, :, :QUART] = (value[:, :QUART] + relay2_f[h].astype(F32)).astype(BF16)
                mid[h, 1, :, QUART:] = value[:, QUART:].astype(BF16)
                flying[h, F2F] = remote(mid.at[h, 1], full2_f.at[h], sems, h, F2F, ahead)
            elif k == 2:
                flying[h, R2B].wait_recv()
                mid[h, 2, :, :QUART] = value[:, :QUART].astype(BF16)
                mid[h, 2, :, QUART:] = (value[:, QUART:] + relay2_b[h].astype(F32)).astype(BF16)
                flying[h, F2B] = remote(mid.at[h, 2], full2_b.at[h], sems, h, F2B, behind)
            else:
                own[:, cols_of(h, "W")] = value

        for k in range(4):
            for h in range(2):
                product(h, k)
                first_sends(h, k)
            if k >= 1:
                for h in range(2):
                    second_sends(h, k - 1)
            if k >= 2:
                for h in range(2):
                    third_sends(h, k - 2)
        for h in range(2):
            second_sends(h, 3)
        fill()
        for k in (2, 3):
            for h in range(2):
                third_sends(h, k)
        for h in range(2):
            flying[h, F2F].wait_recv()
            flying[h, F2B].wait_recv()
        for copy in flying.values():
            copy.wait_send()

    def pages():
        locals_[6].wait()
        locals_[7].wait()
        for t, cache, hbm in ((1, kc, ko_hbm), (2, vc, vo_hbm)):
            for page in range(5):
                value = cache[page]
                for b in range(4):
                    value = jnp.where(look[0, b] == page, qkv[t, b * 128 : (b + 1) * 128, :], value)
                cache[page] = value
            local(12 + t, cache, hbm)

    locals_[0].wait()
    locals_[3].wait()
    reduce_scatter(att, wo, total, pages)

    for h in range(2):
        cs = cols_of(h, "W")
        resid[:, cs] = (
            hid[:, cs].astype(F32) + total[:, cs] + full2_f[h].astype(F32) + full2_b[h].astype(F32)
        )
    locals_[4].wait()
    locals_[5].wait()
    mean = jnp.sum(resid[...], axis=1, keepdims=True) * (1.0 / WIDTH)
    centered = resid[...] - mean
    var = jnp.sum(centered * centered, axis=1, keepdims=True) * (1.0 / WIDTH)
    norm[y, z] = (centered * lax.rsqrt(var + EPS) * gain[...] + bias[...]).astype(BF16)

    flying = {}
    ag = (ag_send, ag_recv)
    OWN_F, OWN_B, REL_F, REL_B = range(4)

    def nview(h, p, s, which):
        a, b = place(h, p, s)
        return norm.at[a, b, :, cols_of(h, which)]

    def ag1(h, i, sp, which, by):
        p, s = prim[h], sec[h]
        ref = nview(h, p, sp, which)
        flying[h, i] = remote(ref, ref, ag, h, i, device(h, p, up1(s, by)))

    def ag2(h, k, i, pp, which, by):
        p, s = prim[h], sec[h]
        ref = nview(h, pp, up1(s, (0, 3, 1, 2)[k]), which)
        flying[h, 4 + 4 * k + i] = remote(ref, ref, ag, h, 4 + 4 * k + i, device(h, up1(p, by), s))

    def ag2_own(h, k):
        ag2(h, k, OWN_F, prim[h], "W", 1)
        ag2(h, k, OWN_B, prim[h], "W", 3)

    def ag2_relay(h, k):
        flying[h, 4 + 4 * k + OWN_F].wait_recv()
        ag2(h, k, REL_F, up1(prim[h], 3), "F", 1)
        flying[h, 4 + 4 * k + OWN_B].wait_recv()
        ag2(h, k, REL_B, up1(prim[h], 1), "B", 3)

    def ag2_done(h, k):
        flying[h, 4 + 4 * k + REL_F].wait_recv()
        flying[h, 4 + 4 * k + REL_B].wait_recv()

    def in_product(h, k):
        sp = up1(sec[h], (0, 3, 1, 2)[k])
        cs = cols_of(h, "W")
        lhs = norm[:, sp, :, cs] if h == 0 else norm[sp, :, :, cs]
        value = nt_dot(lhs.reshape(128, HALF), wi[:, cs]).reshape(4, 32, UNITS)
        if h == 0:
            acc[:, sp] = acc[:, sp] + value
        else:
            acc[sp] = acc[sp] + value

    for h in range(2):
        ag1(h, OWN_F, sec[h], "W", 1)
        ag1(h, OWN_B, sec[h], "W", 3)
    for h in range(2):
        ag2_own(h, 0)

    def fac_wait(i, c):
        fac_copy(0, down_hbm, downs, i).wait()
        fac_copy(1, up_hbm, ups, i).wait()
        return c

    locals_[8].wait()
    locals_[9].wait()
    lax.fori_loop(1, 8, fac_wait, 0)

    for h in range(2):
        flying[h, OWN_F].wait_recv()
        ag1(h, REL_F, up1(sec[h], 3), "F", 1)
        ag2_own(h, 1)
        flying[h, OWN_B].wait_recv()
        ag1(h, REL_B, up1(sec[h], 1), "B", 3)
        ag2_own(h, 2)

    picked = jnp.dot(onehot[...], downs[...].reshape(64 * RANK, 320), preferred_element_type=F32)
    dsel_f[...] = jnp.zeros_like(dsel_f)
    dsel_f[:, :320] = picked
    shifted = jnp.where(lax.rem(m, 2) == 1, pltpu.roll(dsel_f[...], 64, 1), dsel_f[...])
    dsel[...] = shifted.astype(BF16)

    for h in range(2):
        ag2_relay(h, 0)
    for h in range(2):
        flying[h, REL_F].wait_recv()
        flying[h, REL_B].wait_recv()
        ag2_own(h, 3)
    usel[...] = jnp.dot(onehot[...], ups[...].reshape(64 * RANK, UNITS), preferred_element_type=F32).astype(BF16)
    locals_[1].wait()
    for k in range(1, 4):
        for h in range(2):
            ag2_relay(h, k)
        for h in range(2):
            ag2_done(h, k - 1)
            in_product(h, k - 1)
    for h in range(2):
        ag2_done(h, 3)

    window = pl.ds(pl.multiple_of(lax.div(m * 5 - lax.rem(m, 2), 2) * 128, 128), 384)
    ranks = nt_dot(dsel[...], norm[:, :, :, window].reshape(TOK_G, 384))
    token = lax.broadcasted_iota(jnp.int32, (RANK, TOK_G), 1)
    mine = jnp.zeros((RANK, TOK_G), F32)
    for i in range(REQS):
        inside = (token >= starts[i]) & (token < ends[i])
        mine = mine + jnp.where(inside, ranks[i * RANK : (i + 1) * RANK, :], 0.0)
    low[m] = mine.astype(BF16)

    def low_copy(i):
        return pltpu.make_async_remote_copy(
            src_ref=low.at[m],
            dst_ref=low.at[m],
            send_sem=low_send.at[i],
            recv_sem=low_recv.at[i],
            device_id={"mlp": lax.rem(m + i, 16)},
            device_id_type=MESH,
        )

    def low_start(i, c):
        low_copy(i).start()
        return c

    lax.fori_loop(1, 16, low_start, 0)
    for h in range(2):
        in_product(h, 3)

    def low_wait(i, c):
        low_copy(i).wait()
        return c

    lax.fori_loop(1, 16, low_wait, 0)
    lowrank = jnp.sum(low[...].astype(F32), axis=0).astype(BF16).astype(F32)
    for i in range(REQS):
        inside = (token >= starts[i]) & (token < ends[i])
        spread[i * RANK : (i + 1) * RANK, :] = jnp.where(inside, lowrank, 0.0).astype(BF16)

    for i in range(4):
        adapted = lax.dot_general(
            spread[:, i * 128 : (i + 1) * 128], usel[...], (((0,), (0,)), ((), ())), preferred_element_type=F32
        )
        preact = acc[i] + adapted.reshape(4, 32, UNITS)
        act[i] = jax.nn.gelu(preact, approximate=True).astype(BF16)
    for copy in flying.values():
        copy.wait_send()

    def nothing():
        return None

    locals_[2].wait()
    reduce_scatter(act, w2, total, nothing)
    for h in range(2):
        cs = cols_of(h, "W")
        value = resid[:, cs] + (total[:, cs] + full2_f[h].astype(F32) + full2_b[h].astype(F32))
        outb[:, cs] = value.astype(BF16)
    local(15, outb, out_hbm)

    def a2a_sent(i, c):
        for t, ref in enumerate((q_hbm, k_hbm, v_hbm)):
            a2a_copy(t, ref, i).wait_send()
        return c

    lax.fori_loop(1, 16, a2a_sent, 0)
    for i in (13, 14, 15):
        locals_[i].wait()


def shards(*args):
    (queries, keys, values, hidden, w_o, w_in, w_out, gain, bias, down, up, kc, vc, lens, look, adp, slot) = args
    any_, smem = pl.BlockSpec(memory_space=pl.ANY), pl.BlockSpec(memory_space=pltpu.SMEM)
    vmem, dma = pltpu.VMEM, pltpu.SemaphoreType.DMA
    scratch = [
        vmem((3, TOK_G, HEADC), BF16),
        vmem((4, 4, 32, HEADC), BF16),
        vmem((HEADC, WIDTH), BF16),
        vmem((UNITS, WIDTH), BF16),
        vmem((UNITS, WIDTH), BF16),
        vmem((32, WIDTH), BF16),
        vmem((1, WIDTH), F32),
        vmem((1, WIDTH), F32),
        vmem((8, 128, 320), BF16),
        vmem((8, 128, UNITS), BF16),
        vmem((5, 128, HEADC), BF16),
        vmem((5, 128, HEADC), BF16),
        vmem((TOK_G, 1), jnp.int32),
        vmem((4, 4, 32, WIDTH), BF16),
        vmem((4, 4, 32, WIDTH), BF16),
        vmem((2, 4, 32, QUART), BF16),
        vmem((2, 4, 32, QUART), BF16),
        vmem((2, 4, 32, HALF), BF16),
        vmem((2, 4, 32, HALF), BF16),
        vmem((2, 3, 32, HALF), BF16),
        vmem((2, 32, QUART), BF16),
        vmem((2, 32, QUART), BF16),
        vmem((2, 32, HALF), BF16),
        vmem((2, 32, HALF), BF16),
        vmem((32, WIDTH), F32),
        vmem((32, WIDTH), F32),
        vmem((4, 4, 32, UNITS), F32),
        vmem((4, 4, 32, UNITS), BF16),
        vmem((REQS * RANK, 64 * RANK), BF16),
        vmem((REQS * RANK, 384), F32),
        vmem((REQS * RANK, 384), BF16),
        vmem((REQS * RANK, UNITS), BF16),
        vmem((16, RANK, TOK_G), BF16),
        vmem((REQS * RANK, TOK_G), BF16),
        vmem((32, WIDTH), BF16),
        dma((16,)),
        dma((3, 16)),
        dma((3, 16)),
        dma((2, 8)),
        dma((2, 8)),
        dma((16,)),
        dma((16,)),
        dma((2, 28)),
        dma((2, 28)),
        dma((2, 20)),
        dma((2, 20)),
    ]
    return pl.pallas_call(
        kernel,
        out_shape=(
            jax.ShapeDtypeStruct((32, WIDTH), BF16),
            jax.ShapeDtypeStruct((5, 128, HEADC), BF16),
            jax.ShapeDtypeStruct((5, 128, HEADC), BF16),
        ),
        in_specs=[any_] * 13 + [smem] * 4,
        out_specs=(any_, any_, any_),
        scratch_shapes=scratch,
        compiler_params=pltpu.CompilerParams(
            collective_id=0, has_side_effects=True, vmem_limit_bytes=62 * 1024 * 1024
        ),
    )(
        queries, keys, values, hidden, w_o, w_in.T, w_out, gain.reshape(1, WIDTH), bias.reshape(1, WIDTH),
        jnp.transpose(down, (0, 2, 1)).reshape(128, 320), up.reshape(128, UNITS), kc, vc, lens, look, adp, slot,
    )


def solution(mesh):
    in_specs = (
        P(("req", "mlp"), None),
        P(("req", "mlp"), None),
        P(("req", "mlp"), None),
        P(("req", "mlp"), None),
        P("mlp", None),
        P(None, "mlp"),
        P("mlp", None),
        P(),
        P(),
        P("req", "mlp", None),
        P("req", None, "mlp"),
        P("req", None, "mlp"),
        P("req", None, "mlp"),
        P("req", None),
        P("req", None),
        P("req", None),
        P(),
    )
    out_specs = (P(("req", "mlp"), None), P("req", None, "mlp"), P("req", None, "mlp"))
    return jax.shard_map(shards, mesh=mesh, in_specs=in_specs, out_specs=out_specs, check_vma=False)
```

```python
import functools

import jax
import jax.numpy as jnp
from jax import lax
from jax.experimental import pallas as pl
from jax.experimental.pallas import tpu as pltpu
from jax.sharding import PartitionSpec as P

MESH = pl.DeviceIdType.MESH
HS = 128
RANK = 16
REQS = 16
TOK_G = 512
WIDTH = 5120
HALF = WIDTH // 2
QUART = HALF // 2
UNITS = 864
HEADC = 256
TILE = 512
EPS = 1e-06
F32 = jnp.float32
BF16 = jnp.bfloat16

RELAY_F, RELAY_B, FULL = range(3)
R2F, R2B, FULL2 = range(12, 15)


def nt_dot(a, b):
    return lax.dot_general(a, b, (((1,), (1,)), ((), ())), preferred_element_type=F32)


def kernel(
    q_hbm, k_hbm, v_hbm, hid_hbm, wo_hbm, wi_hbm, w2_hbm, gain_hbm, bias_hbm, down_hbm, up_hbm, kc_hbm, vc_hbm,
    lens, look, adp, slot,
    outb, ko, vo,
    qkv, att, wo, wi, w2, hid, gain, bias, downs, ups, kc, vc, start_col,
    part, norm, relay_f, relay_b, full_f, full_b, mid, relay2_f, relay2_b, full2_f, full2_b,
    resid, total, acc, act, onehot, dsel_f, dsel, usel, low, spread,
    local_sem, a2a_send, a2a_recv, fac_send, fac_recv, low_send, low_recv, rs_send, rs_recv, ag_send, ag_recv,
):
    m = lax.axis_index("mlp")
    r = lax.axis_index("req")
    y, z = lax.div(m, 4), lax.rem(m, 4)

    def place(h, p, s):
        return (p, s) if h == 0 else (s, p)

    def device(h, p, s):
        a, b = place(h, p, s)
        return {"mlp": a * 4 + b}

    prim = (y, z)
    sec = (z, y)

    def up1(i, by):
        return lax.rem(i + by, 4)

    def wait_for(like, sem):
        pltpu.make_async_copy(like, like, sem).wait()

    locals_ = {}

    def local(i, src, dst):
        c = pltpu.make_async_copy(src, dst, local_sem.at[i])
        c.start()
        locals_[i] = c

    local(0, wo_hbm, wo)
    local(3, hid_hbm, hid)
    local(4, gain_hbm, gain)
    local(5, bias_hbm, bias)
    local(6, kc_hbm, kc)
    local(7, vc_hbm, vc)
    pltpu.make_async_copy(down_hbm, downs.at[r], fac_recv.at[0]).start()
    pltpu.make_async_copy(up_hbm, ups.at[r], fac_recv.at[1]).start()
    for t, ref in enumerate((q_hbm, k_hbm, v_hbm)):
        cols = pl.ds(pl.multiple_of(m * HEADC, HEADC), HEADC)
        rows = pl.ds(pl.multiple_of(m * 32, 32), 32)
        pltpu.make_async_copy(ref.at[:, cols], qkv.at[t, rows, :], a2a_recv.at[0]).start()

    barrier = pltpu.get_barrier_semaphore()

    def greet_mlp(i, c):
        pl.semaphore_signal(barrier, inc=1, device_id={"mlp": lax.rem(m + i, 16)}, device_id_type=MESH)
        return c

    def greet_req(i, c):
        pl.semaphore_signal(barrier, inc=1, device_id={"req": lax.rem(r + i, 8)}, device_id_type=MESH)
        return c

    lax.fori_loop(1, 16, greet_mlp, 0)
    lax.fori_loop(1, 8, greet_req, 0)
    pl.semaphore_wait(barrier, 22)

    def a2a_copy(t, ref, i):
        d = lax.rem(m + i, 16)
        return pltpu.make_async_remote_copy(
            src_ref=ref.at[:, pl.ds(pl.multiple_of(d * HEADC, HEADC), HEADC)],
            dst_ref=qkv.at[t, pl.ds(pl.multiple_of(m * 32, 32), 32), :],
            send_sem=a2a_send.at[0],
            recv_sem=a2a_recv.at[0],
            device_id={"mlp": d},
            device_id_type=MESH,
        )

    def a2a_start(i, c):
        for t, ref in enumerate((q_hbm, k_hbm, v_hbm)):
            a2a_copy(t, ref, i).start()
        return c

    lax.fori_loop(1, 16, a2a_start, 0)

    def fac_copy(t, src, dst, i):
        return pltpu.make_async_remote_copy(
            src_ref=src,
            dst_ref=dst.at[r],
            send_sem=fac_send.at[t],
            recv_sem=fac_recv.at[t],
            device_id={"req": lax.rem(r + i, 8)},
            device_id_type=MESH,
        )

    def fac_start(i, c):
        fac_copy(0, down_hbm, downs, i).start()
        fac_copy(1, up_hbm, ups, i).start()
        return c

    lax.fori_loop(1, 8, fac_start, 0)
    local(1, wi_hbm, wi)
    local(2, w2_hbm, w2)

    pos = lax.broadcasted_iota(jnp.int32, (TOK_G, 1), 0)
    starts, ends = [], []
    first = jnp.zeros((TOK_G, 1), jnp.int32)
    end = jnp.int32(0)
    for i in range(REQS):
        starts.append(end)
        end = end + lens[0, i]
        ends.append(end)
        first = jnp.where(pos >= end, end, first)
    start_col[...] = first

    for i in range(REQS):
        wanted = slot[adp[0, i]] * RANK
        lane = lax.broadcasted_iota(jnp.int32, (RANK, 64 * RANK), 1)
        sub = lax.broadcasted_iota(jnp.int32, (RANK, 64 * RANK), 0)
        onehot[i * RANK : (i + 1) * RANK, :] = (lane - sub == wanted).astype(F32).astype(BF16)
    acc[...] = jnp.zeros_like(acc)

    wait_for(qkv, a2a_recv.at[0])

    for h in range(2):
        hc = slice(h * HS, (h + 1) * HS)
        for i in range(4):
            rows, length = slice(i * 128, (i + 1) * 128), (i + 1) * 128
            score = nt_dot(qkv[0, rows, hc], qkv[1, :length, hc]) * (HS ** (-0.5))
            qi = lax.broadcasted_iota(jnp.int32, (128, length), 0) + i * 128
            kj = lax.broadcasted_iota(jnp.int32, (128, length), 1)
            allowed = (kj <= qi) & (kj >= start_col[rows, :])
            score = jnp.where(allowed, score, -1e30)
            expo = jnp.exp(score - jnp.max(score, axis=1, keepdims=True))
            weights = (expo / jnp.sum(expo, axis=1, keepdims=True)).astype(BF16)
            mixed = jnp.dot(weights, qkv[2, :length, hc], preferred_element_type=F32)
            att[i, :, :, hc] = mixed.astype(BF16).reshape(4, 32, HS)

    def remote(src, dst, sems, h, i, dev):
        c = pltpu.make_async_remote_copy(
            src_ref=src,
            dst_ref=dst,
            send_sem=sems[0].at[h],
            recv_sem=sems[1].at[h, i],
            device_id=dev,
            device_id_type=MESH,
        )
        c.start()
        return c

    def cols_of(h, which):
        base = h * HALF
        if which == "F":
            return slice(base, base + QUART)
        if which == "B":
            return slice(base + QUART, base + HALF)
        return slice(base, base + HALF)

    def reduce_scatter(left, right, own, fill):
        flying = {}
        sems = (rs_send, rs_recv)

        def view(h, p, s, which):
            a, b = place(h, p, s)
            return part.at[a, b, :, cols_of(h, which)]

        def load(h, p, s, which):
            a, b = place(h, p, s)
            return part[a, b, :, cols_of(h, which)].astype(F32)

        def store(h, p, s, which, value):
            a, b = place(h, p, s)
            part[a, b, :, cols_of(h, which)] = value.astype(BF16)

        def order(h, k):
            return up1(sec[h], (2, 1, 3, 0)[k])

        def product(h, k):
            s = order(h, k)
            lhs = left[:, s] if h == 0 else left[s]
            lhs = lhs.reshape(128, left.shape[3])
            for c in range(h * HALF, (h + 1) * HALF, TILE):
                value = jnp.dot(lhs, right[:, c : c + TILE], preferred_element_type=F32).astype(BF16)
                value = value.reshape(4, 32, TILE)
                if h == 0:
                    part[:, s, :, c : c + TILE] = value
                else:
                    part[s, :, :, c : c + TILE] = value

        def first_sends(h, k):
            p, s, sp = prim[h], sec[h], order(h, k)
            ahead, behind = device(h, up1(p, 1), s), device(h, up1(p, 3), s)
            i = 3 * k
            far = up1(p, 2)
            flying[h, i + RELAY_F] = remote(view(h, far, sp, "F"), relay_f.at[h, k], sems, h, i + RELAY_F, ahead)
            flying[h, i + RELAY_B] = remote(view(h, far, sp, "B"), relay_b.at[h, k], sems, h, i + RELAY_B, behind)
            remote(view(h, up1(p, 1), sp, "B"), full_f.at[h, k, :, QUART:], sems, h, i + FULL, ahead)
            remote(view(h, up1(p, 3), sp, "F"), full_b.at[h, k, :, :QUART], sems, h, i + FULL, behind)

        def second_sends(h, k):
            p, s, sp = prim[h], sec[h], order(h, k)
            ahead, behind = device(h, up1(p, 1), s), device(h, up1(p, 3), s)
            i = 3 * k
            flying[h, i + RELAY_F].wait_recv()
            store(h, up1(p, 1), sp, "F", load(h, up1(p, 1), sp, "F") + relay_f[h, k].astype(F32))
            remote(view(h, up1(p, 1), sp, "F"), full_f.at[h, k, :, :QUART], sems, h, i + FULL, ahead)
            flying[h, i + RELAY_B].wait_recv()
            store(h, up1(p, 3), sp, "B", load(h, up1(p, 3), sp, "B") + relay_b[h, k].astype(F32))
            remote(view(h, up1(p, 3), sp, "B"), full_b.at[h, k, :, QUART:], sems, h, i + FULL, behind)

        def third_sends(h, k):
            p, s, sp = prim[h], sec[h], order(h, k)
            wait_for(wo.at[0:32], rs_recv.at[h, 3 * k + FULL])
            value = load(h, p, sp, "W") + full_f[h, k].astype(F32) + full_b[h, k].astype(F32)
            ahead, behind = device(h, p, up1(s, 1)), device(h, p, up1(s, 3))
            if k == 0:
                mid[h, 0] = value.astype(BF16)
                flying[h, R2F] = remote(mid.at[h, 0, :, :QUART], relay2_f.at[h], sems, h, R2F, ahead)
                flying[h, R2B] = remote(mid.at[h, 0, :, QUART:], relay2_b.at[h], sems, h, R2B, behind)
            elif k == 1:
                flying[h, R2F].wait_recv()
                mid[h, 1, :, :QUART] = (value[:, :QUART] + relay2_f[h].astype(F32)).astype(BF16)
                mid[h, 1, :, QUART:] = value[:, QUART:].astype(BF16)
                remote(mid.at[h, 1], full2_f.at[h], sems, h, FULL2, ahead)
            elif k == 2:
                flying[h, R2B].wait_recv()
                mid[h, 2, :, :QUART] = value[:, :QUART].astype(BF16)
                mid[h, 2, :, QUART:] = (value[:, QUART:] + relay2_b[h].astype(F32)).astype(BF16)
                remote(mid.at[h, 2], full2_b.at[h], sems, h, FULL2, behind)
            else:
                own[:, cols_of(h, "W")] = value

        for k in range(4):
            for h in range(2):
                product(h, k)
                first_sends(h, k)
            if k >= 1:
                for h in range(2):
                    second_sends(h, k - 1)
            if k >= 2:
                for h in range(2):
                    third_sends(h, k - 2)
        for h in range(2):
            second_sends(h, 3)
        fill()
        for k in (2, 3):
            for h in range(2):
                third_sends(h, k)
        for h in range(2):
            wait_for(wo.at[0:32], rs_recv.at[h, FULL2])
        for h in range(2):
            wait_for(wo.at[0:240], rs_send.at[h])

    def pages():
        locals_[6].wait()
        locals_[7].wait()
        for t, cache, out in ((1, kc, ko), (2, vc, vo)):
            for page in range(5):
                value = cache[page]
                for b in range(4):
                    value = jnp.where(look[0, b] == page, qkv[t, b * 128 : (b + 1) * 128, :], value)
                out[page] = value

    locals_[0].wait()
    locals_[3].wait()
    reduce_scatter(att, wo, total, pages)

    for h in range(2):
        cs = cols_of(h, "W")
        resid[:, cs] = (
            hid[:, cs].astype(F32) + total[:, cs] + full2_f[h].astype(F32) + full2_b[h].astype(F32)
        )
    locals_[4].wait()
    locals_[5].wait()
    mean = jnp.sum(resid[...], axis=1, keepdims=True) * (1.0 / WIDTH)
    centered = resid[...] - mean
    var = jnp.sum(centered * centered, axis=1, keepdims=True) * (1.0 / WIDTH)
    norm[y, z] = (centered * lax.rsqrt(var + EPS) * gain[...] + bias[...]).astype(BF16)

    flying = {}
    ag = (ag_send, ag_recv)
    OWN_F, OWN_B, REL = range(3)

    def nview(h, p, s, which):
        a, b = place(h, p, s)
        return norm.at[a, b, :, cols_of(h, which)]

    def ag1(h, i, sp, which, by):
        p, s = prim[h], sec[h]
        ref = nview(h, p, sp, which)
        flying[h, i] = remote(ref, ref, ag, h, i, device(h, p, up1(s, by)))

    def ag2(h, k, i, pp, which, by):
        p, s = prim[h], sec[h]
        ref = nview(h, pp, up1(s, (0, 3, 1, 2)[k]), which)
        flying[h, 3 + 3 * k + i] = remote(ref, ref, ag, h, 3 + 3 * k + i, device(h, up1(p, by), s))

    def ag2_own(h, k):
        ag2(h, k, OWN_F, prim[h], "W", 1)
        ag2(h, k, OWN_B, prim[h], "W", 3)

    def ag2_relay(h, k):
        flying[h, 3 + 3 * k + OWN_F].wait_recv()
        ag2(h, k, REL, up1(prim[h], 3), "F", 1)
        flying[h, 3 + 3 * k + OWN_B].wait_recv()
        ag2(h, k, REL, up1(prim[h], 1), "B", 3)

    def ag2_done(h, k):
        wait_for(wo.at[0:16], ag_recv.at[h, 3 + 3 * k + REL])

    def in_product(h, k):
        sp = up1(sec[h], (0, 3, 1, 2)[k])
        cs = cols_of(h, "W")
        lhs = norm[:, sp, :, cs] if h == 0 else norm[sp, :, :, cs]
        value = nt_dot(lhs.reshape(128, HALF), wi[:, cs]).reshape(4, 32, UNITS)
        if h == 0:
            acc[:, sp] = acc[:, sp] + value
        else:
            acc[sp] = acc[sp] + value

    for h in range(2):
        ag1(h, OWN_F, sec[h], "W", 1)
        ag1(h, OWN_B, sec[h], "W", 3)
    for h in range(2):
        ag2_own(h, 0)

    for t, ref in enumerate((downs, ups)):
        wait_for(ref, fac_recv.at[t])
        wait_for(ref.at[0:7], fac_send.at[t])

    for h in range(2):
        flying[h, OWN_F].wait_recv()
        ag1(h, REL, up1(sec[h], 3), "F", 1)
        ag2_own(h, 1)
        flying[h, OWN_B].wait_recv()
        ag1(h, REL, up1(sec[h], 1), "B", 3)
        ag2_own(h, 2)

    picked = jnp.dot(onehot[...], downs[...].reshape(64 * RANK, 320), preferred_element_type=F32)
    dsel_f[...] = jnp.zeros_like(dsel_f)
    dsel_f[:, :320] = picked
    shifted = jnp.where(lax.rem(m, 2) == 1, pltpu.roll(dsel_f[...], 64, 1), dsel_f[...])
    dsel[...] = shifted.astype(BF16)

    for h in range(2):
        ag2_relay(h, 0)
    for h in range(2):
        wait_for(wo.at[0:16], ag_recv.at[h, REL])
        ag2_own(h, 3)
    usel[...] = jnp.dot(onehot[...], ups[...].reshape(64 * RANK, UNITS), preferred_element_type=F32).astype(BF16)
    locals_[1].wait()
    for k in range(1, 4):
        for h in range(2):
            ag2_relay(h, k)
        for h in range(2):
            ag2_done(h, k - 1)
            in_product(h, k - 1)
    for h in range(2):
        ag2_done(h, 3)

    window = pl.ds(pl.multiple_of(lax.div(m * 5 - lax.rem(m, 2), 2) * 128, 128), 384)
    ranks = nt_dot(dsel[...], norm[:, :, :, window].reshape(TOK_G, 384))
    token = lax.broadcasted_iota(jnp.int32, (RANK, TOK_G), 1)
    mine = jnp.zeros((RANK, TOK_G), F32)
    for i in range(REQS):
        inside = (token >= starts[i]) & (token < ends[i])
        mine = mine + jnp.where(inside, ranks[i * RANK : (i + 1) * RANK, :], 0.0)
    low[m] = mine.astype(BF16)

    def low_copy(i):
        return pltpu.make_async_remote_copy(
            src_ref=low.at[m],
            dst_ref=low.at[m],
            send_sem=low_send.at[0],
            recv_sem=low_recv.at[0],
            device_id={"mlp": lax.rem(m + i, 16)},
            device_id_type=MESH,
        )

    def low_start(i, c):
        low_copy(i).start()
        return c

    lax.fori_loop(1, 16, low_start, 0)
    for h in range(2):
        in_product(h, 3)

    wait_for(low.at[0:15], low_recv.at[0])
    wait_for(low.at[0:15], low_send.at[0])
    lowrank = jnp.sum(low[...].astype(F32), axis=0).astype(BF16).astype(F32)
    for i in range(REQS):
        inside = (token >= starts[i]) & (token < ends[i])
        spread[i * RANK : (i + 1) * RANK, :] = jnp.where(inside, lowrank, 0.0).astype(BF16)

    for i in range(4):
        adapted = lax.dot_general(
            spread[:, i * 128 : (i + 1) * 128], usel[...], (((0,), (0,)), ((), ())), preferred_element_type=F32
        )
        preact = acc[i] + adapted.reshape(4, 32, UNITS)
        act[i] = jax.nn.gelu(preact, approximate=True).astype(BF16)
    for h in range(2):
        wait_for(wo.at[0:240], ag_send.at[h])

    def nothing():
        return None

    locals_[2].wait()
    reduce_scatter(act, w2, total, nothing)
    for h in range(2):
        cs = cols_of(h, "W")
        value = resid[:, cs] + (total[:, cs] + full2_f[h].astype(F32) + full2_b[h].astype(F32))
        outb[:, cs] = value.astype(BF16)

    wait_for(qkv.at[:, 0:480], a2a_send.at[0])


def shards(*args):
    (queries, keys, values, hidden, w_o, w_in, w_out, gain, bias, down, up, kc, vc, lens, look, adp, slot) = args
    any_, smem = pl.BlockSpec(memory_space=pl.ANY), pl.BlockSpec(memory_space=pltpu.SMEM)
    vmem, dma = pltpu.VMEM, pltpu.SemaphoreType.DMA
    scratch = [
        vmem((3, TOK_G, HEADC), BF16),
        vmem((4, 4, 32, HEADC), BF16),
        vmem((HEADC, WIDTH), BF16),
        vmem((UNITS, WIDTH), BF16),
        vmem((UNITS, WIDTH), BF16),
        vmem((32, WIDTH), BF16),
        vmem((1, WIDTH), F32),
        vmem((1, WIDTH), F32),
        vmem((8, 128, 320), BF16),
        vmem((8, 128, UNITS), BF16),
        vmem((5, 128, HEADC), BF16),
        vmem((5, 128, HEADC), BF16),
        vmem((TOK_G, 1), jnp.int32),
        vmem((4, 4, 32, WIDTH), BF16),
        vmem((4, 4, 32, WIDTH), BF16),
        vmem((2, 4, 32, QUART), BF16),
        vmem((2, 4, 32, QUART), BF16),
        vmem((2, 4, 32, HALF), BF16),
        vmem((2, 4, 32, HALF), BF16),
        vmem((2, 3, 32, HALF), BF16),
        vmem((2, 32, QUART), BF16),
        vmem((2, 32, QUART), BF16),
        vmem((2, 32, HALF), BF16),
        vmem((2, 32, HALF), BF16),
        vmem((32, WIDTH), F32),
        vmem((32, WIDTH), F32),
        vmem((4, 4, 32, UNITS), F32),
        vmem((4, 4, 32, UNITS), BF16),
        vmem((REQS * RANK, 64 * RANK), BF16),
        vmem((REQS * RANK, 384), F32),
        vmem((REQS * RANK, 384), BF16),
        vmem((REQS * RANK, UNITS), BF16),
        vmem((16, RANK, TOK_G), BF16),
        vmem((REQS * RANK, TOK_G), BF16),
        dma((8,)),
        dma((1,)),
        dma((1,)),
        dma((2,)),
        dma((2,)),
        dma((1,)),
        dma((1,)),
        dma((2,)),
        dma((2, 15)),
        dma((2,)),
        dma((2, 15)),
    ]
    return pl.pallas_call(
        kernel,
        out_shape=(
            pltpu.VMEM((32, WIDTH), BF16),
            pltpu.VMEM((5, 128, HEADC), BF16),
            pltpu.VMEM((5, 128, HEADC), BF16),
        ),
        in_specs=[any_] * 13 + [smem] * 4,
        out_specs=(pl.BlockSpec(memory_space=pltpu.VMEM),) * 3,
        scratch_shapes=scratch,
        compiler_params=pltpu.CompilerParams(
            collective_id=0, has_side_effects=True, vmem_limit_bytes=62 * 1024 * 1024
        ),
    )(
        queries, keys, values, hidden, w_o, w_in.T, w_out, gain.reshape(1, WIDTH), bias.reshape(1, WIDTH),
        jnp.transpose(down, (0, 2, 1)).reshape(128, 320), up.reshape(128, UNITS), kc, vc, lens, look, adp, slot,
    )


def solution(mesh):
    in_specs = (
        P(("req", "mlp"), None),
        P(("req", "mlp"), None),
        P(("req", "mlp"), None),
        P(("req", "mlp"), None),
        P("mlp", None),
        P(None, "mlp"),
        P("mlp", None),
        P(),
        P(),
        P("req", "mlp", None),
        P("req", None, "mlp"),
        P("req", None, "mlp"),
        P("req", None, "mlp"),
        P("req", None),
        P("req", None),
        P("req", None),
        P(),
    )
    out_specs = (P(("req", "mlp"), None), P("req", None, "mlp"), P("req", None, "mlp"))
    return jax.shard_map(shards, mesh=mesh, in_specs=in_specs, out_specs=out_specs, check_vma=False)
```

```python
import functools

import jax
import jax.numpy as jnp
from jax import lax
from jax.experimental import pallas as pl
from jax.experimental.pallas import tpu as pltpu
from jax.sharding import PartitionSpec as P

MESH = pl.DeviceIdType.MESH
HS = 128
RANK = 16
REQS = 16
TOK_G = 512
WIDTH = 5120
HALF = WIDTH // 2
QUART = HALF // 2
UNITS = 864
HEADC = 256
TILE = 512
EPS = 1e-06
F32 = jnp.float32
BF16 = jnp.bfloat16

RELAY_F, RELAY_B, FULL = range(3)
R2F, R2B, FULL2 = range(12, 15)
OWN_F, OWN_B, REL = range(3)


def nt_dot(a, b):
    return lax.dot_general(a, b, (((1,), (1,)), ((), ())), preferred_element_type=F32)


def kernel(
    q_hbm, k_hbm, v_hbm, hid_hbm, wo_hbm, wi_hbm, w2_hbm, gain_hbm, bias_hbm, down_hbm, up_hbm, kc_hbm, vc_hbm,
    lens, look, adp, slot,
    outb, ko, vo,
    qkv, att, wo, wi, w2, hid, gain, bias, downs, ups, kc, vc, start_col,
    part, norm, relay_f, relay_b, full_f, full_b, mid, relay2_f, relay2_b, full2_f, full2_b,
    resid, total, acc, act, onehot, dsel_f, dsel, usel, low, spread,
    local_sem, a2a_send, a2a_recv, fac_send, fac_recv, low_send, low_recv, rs_send, rs_recv, ag_send, ag_recv,
):
    m = lax.axis_index("mlp")
    r = lax.axis_index("req")
    y, z = lax.div(m, 4), lax.rem(m, 4)

    def place(h, p, s):
        return (p, s) if h == 0 else (s, p)

    def device(h, p, s):
        a, b = place(h, p, s)
        return {"mlp": a * 4 + b}

    prim = (y, z)
    sec = (z, y)

    def up1(i, by):
        return lax.rem(i + by, 4)

    def wait_for(like, sem):
        pltpu.make_async_copy(like, like, sem).wait()

    locals_ = {}

    def local(i, src, dst):
        c = pltpu.make_async_copy(src, dst, local_sem.at[i])
        c.start()
        locals_[i] = c

    local(0, wo_hbm, wo)
    local(3, hid_hbm, hid)
    local(4, gain_hbm, gain)
    local(5, bias_hbm, bias)
    local(6, kc_hbm, kc)
    local(7, vc_hbm, vc)
    pltpu.make_async_copy(down_hbm, downs.at[r], fac_recv.at[0]).start()
    pltpu.make_async_copy(up_hbm, ups.at[r], fac_recv.at[1]).start()
    own_rows = pl.ds(pl.multiple_of(m * 32, 32), 32)
    for h in range(2):
        for t, ref in enumerate((q_hbm, k_hbm, v_hbm)):
            cols = pl.ds(pl.multiple_of(m * HEADC + h * HS, HS), HS)
            mine = qkv.at[t, own_rows, h * HS : (h + 1) * HS]
            pltpu.make_async_copy(ref.at[:, cols], mine, a2a_recv.at[h]).start()

    barrier = pltpu.get_barrier_semaphore()

    def greet_mlp(i, c):
        pl.semaphore_signal(barrier, inc=1, device_id={"mlp": lax.rem(m + i, 16)}, device_id_type=MESH)
        return c

    def greet_req(i, c):
        pl.semaphore_signal(barrier, inc=1, device_id={"req": lax.rem(r + i, 8)}, device_id_type=MESH)
        return c

    lax.fori_loop(1, 16, greet_mlp, 0)
    lax.fori_loop(1, 8, greet_req, 0)
    pl.semaphore_wait(barrier, 22)

    def a2a_copy(h, t, ref, i):
        d = lax.rem(m + i, 16)
        return pltpu.make_async_remote_copy(
            src_ref=ref.at[:, pl.ds(pl.multiple_of(d * HEADC + h * HS, HS), HS)],
            dst_ref=qkv.at[t, own_rows, h * HS : (h + 1) * HS],
            send_sem=a2a_send.at[0],
            recv_sem=a2a_recv.at[h],
            device_id={"mlp": d},
            device_id_type=MESH,
        )

    for h in range(2):

        def a2a_start(i, c, h=h):
            for t, ref in enumerate((q_hbm, k_hbm, v_hbm)):
                a2a_copy(h, t, ref, i).start()
            return c

        lax.fori_loop(1, 16, a2a_start, 0)

    def fac_copy(t, src, dst, i):
        return pltpu.make_async_remote_copy(
            src_ref=src,
            dst_ref=dst.at[r],
            send_sem=fac_send.at[t],
            recv_sem=fac_recv.at[t],
            device_id={"req": lax.rem(r + i, 8)},
            device_id_type=MESH,
        )

    def fac_start(i, c):
        fac_copy(0, down_hbm, downs, i).start()
        fac_copy(1, up_hbm, ups, i).start()
        return c

    lax.fori_loop(1, 8, fac_start, 0)
    local(1, wi_hbm, wi)
    local(2, w2_hbm, w2)

    pos = lax.broadcasted_iota(jnp.int32, (TOK_G, 1), 0)
    starts, ends = [], []
    first = jnp.zeros((TOK_G, 1), jnp.int32)
    end = jnp.int32(0)
    for i in range(REQS):
        starts.append(end)
        end = end + lens[0, i]
        ends.append(end)
        first = jnp.where(pos >= end, end, first)
    start_col[...] = first

    for i in range(REQS):
        wanted = slot[adp[0, i]] * RANK
        lane = lax.broadcasted_iota(jnp.int32, (RANK, 64 * RANK), 1)
        sub = lax.broadcasted_iota(jnp.int32, (RANK, 64 * RANK), 0)
        onehot[i * RANK : (i + 1) * RANK, :] = (lane - sub == wanted).astype(F32).astype(BF16)
    acc[...] = jnp.zeros_like(acc)


    for h in range(2):
        hc = slice(h * HS, (h + 1) * HS)
        wait_for(qkv.at[:, :, hc], a2a_recv.at[h])
        for i in range(4):
            rows, length = slice(i * 128, (i + 1) * 128), (i + 1) * 128
            score = nt_dot(qkv[0, rows, hc], qkv[1, :length, hc]) * (HS ** (-0.5))
            qi = lax.broadcasted_iota(jnp.int32, (128, length), 0) + i * 128
            kj = lax.broadcasted_iota(jnp.int32, (128, length), 1)
            allowed = (kj <= qi) & (kj >= start_col[rows, :])
            score = jnp.where(allowed, score, -1e30)
            expo = jnp.exp(score - jnp.max(score, axis=1, keepdims=True))
            weights = (expo / jnp.sum(expo, axis=1, keepdims=True)).astype(BF16)
            mixed = jnp.dot(weights, qkv[2, :length, hc], preferred_element_type=F32)
            att[i, :, :, hc] = mixed.astype(BF16).reshape(4, 32, HS)

    def remote(src, dst, sems, t, h, i, dev):
        c = pltpu.make_async_remote_copy(
            src_ref=src,
            dst_ref=dst,
            send_sem=sems[0].at[t, h],
            recv_sem=sems[1].at[t, h, i],
            device_id=dev,
            device_id_type=MESH,
        )
        c.start()

    def rows_of(t):
        return slice(16 * t, 16 * t + 16)

    def cols_of(h, which):
        base = h * HALF
        if which == "F":
            return slice(base, base + QUART)
        if which == "B":
            return slice(base + QUART, base + HALF)
        return slice(base, base + HALF)

    UNIT, PIECE, PAIR, SENT = wo.at[0:16, :QUART], wo.at[0:16, :HALF], wo.at[0:16], wo.at[0:240, :HALF]

    class Scatter:
        def __init__(self, t, left, right):
            self.t, self.left, self.right = t, left, right
            self.sems = (rs_send, rs_recv)

        def at(self, h, p, s, which):
            a, b = place(h, p, s)
            return (a, b, rows_of(self.t), cols_of(h, which))

        def order(self, h, k):
            return up1(sec[h], (2, 1, 3, 0)[k])

        def product(self, h, k):
            s, rows = self.order(h, k), rows_of(self.t)
            left, right = self.left, self.right
            lhs = left[:, s, rows] if h == 0 else left[s, :, rows]
            lhs = lhs.reshape(64, left.shape[3])
            for c in range(h * HALF, (h + 1) * HALF, TILE):
                value = jnp.dot(lhs, right[:, c : c + TILE], preferred_element_type=F32).astype(BF16)
                value = value.reshape(4, 16, TILE)
                if h == 0:
                    part[:, s, rows, c : c + TILE] = value
                else:
                    part[s, :, rows, c : c + TILE] = value

        def first(self, k):
            t, rows, sems = self.t, rows_of(self.t), self.sems
            for h in range(2):
                self.product(h, k)
                p, s, sp = prim[h], sec[h], self.order(h, k)
                ahead, behind = device(h, up1(p, 1), s), device(h, up1(p, 3), s)
                far, i = up1(p, 2), 3 * k
                remote(part.at[self.at(h, far, sp, "F")], relay_f.at[h, k, rows], sems, t, h, i + RELAY_F, ahead)
                remote(part.at[self.at(h, far, sp, "B")], relay_b.at[h, k, rows], sems, t, h, i + RELAY_B, behind)
                remote(part.at[self.at(h, up1(p, 1), sp, "B")], full_f.at[h, k, rows, QUART:], sems, t, h, i + FULL, ahead)
                remote(part.at[self.at(h, up1(p, 3), sp, "F")], full_b.at[h, k, rows, :QUART], sems, t, h, i + FULL, behind)

        def second(self, k):
            t, rows, sems = self.t, rows_of(self.t), self.sems
            for h in range(2):
                p, s, sp = prim[h], sec[h], self.order(h, k)
                ahead, behind = device(h, up1(p, 1), s), device(h, up1(p, 3), s)
                i = 3 * k
                wait_for(UNIT, rs_recv.at[t, h, i + RELAY_F])
                at = self.at(h, up1(p, 1), sp, "F")
                part[at] = (part[at].astype(F32) + relay_f[h, k, rows].astype(F32)).astype(BF16)
                remote(part.at[at], full_f.at[h, k, rows, :QUART], sems, t, h, i + FULL, ahead)
                wait_for(UNIT, rs_recv.at[t, h, i + RELAY_B])
                at = self.at(h, up1(p, 3), sp, "B")
                part[at] = (part[at].astype(F32) + relay_b[h, k, rows].astype(F32)).astype(BF16)
                remote(part.at[at], full_b.at[h, k, rows, QUART:], sems, t, h, i + FULL, behind)

        def third(self, k):
            t, rows, sems = self.t, rows_of(self.t), self.sems
            for h in range(2):
                p, s, sp = prim[h], sec[h], self.order(h, k)
                wait_for(PAIR, rs_recv.at[t, h, 3 * k + FULL])
                value = (
                    part[self.at(h, p, sp, "W")].astype(F32)
                    + full_f[h, k, rows].astype(F32)
                    + full_b[h, k, rows].astype(F32)
                )
                ahead, behind = device(h, p, up1(s, 1)), device(h, p, up1(s, 3))
                if k == 0:
                    mid[h, 0, rows] = value.astype(BF16)
                    remote(mid.at[h, 0, rows, :QUART], relay2_f.at[h, rows], sems, t, h, R2F, ahead)
                    remote(mid.at[h, 0, rows, QUART:], relay2_b.at[h, rows], sems, t, h, R2B, behind)
                elif k == 1:
                    wait_for(UNIT, rs_recv.at[t, h, R2F])
                    mid[h, 1, rows, :QUART] = (value[:, :QUART] + relay2_f[h, rows].astype(F32)).astype(BF16)
                    mid[h, 1, rows, QUART:] = value[:, QUART:].astype(BF16)
                    remote(mid.at[h, 1, rows], full2_f.at[h, rows], sems, t, h, FULL2, ahead)
                elif k == 2:
                    wait_for(UNIT, rs_recv.at[t, h, R2B])
                    mid[h, 2, rows, :QUART] = value[:, :QUART].astype(BF16)
                    mid[h, 2, rows, QUART:] = (value[:, QUART:] + relay2_b[h, rows].astype(F32)).astype(BF16)
                    remote(mid.at[h, 2, rows], full2_b.at[h, rows], sems, t, h, FULL2, behind)
                else:
                    total[rows, cols_of(h, "W")] = value

        def last(self):
            rows = rows_of(self.t)
            for h in range(2):
                wait_for(PAIR, rs_recv.at[self.t, h, FULL2])
                wait_for(SENT, rs_send.at[self.t, h])
            return [
                total[rows, cols_of(h, "W")] + full2_f[h, rows].astype(F32) + full2_b[h, rows].astype(F32)
                for h in range(2)
            ]

    class Gather:
        def __init__(self, t):
            self.t = t
            self.sems = (ag_send, ag_recv)

        def order(self, h, k):
            return up1(sec[h], (0, 3, 1, 2)[k])

        def put(self, h, i, pp, sp, which, dev):
            a, b = place(h, pp, sp)
            ref = norm.at[a, b, rows_of(self.t), cols_of(h, which)]
            remote(ref, ref, self.sems, self.t, h, i, dev)

        def one(self, h, i, sp, which, by):
            self.put(h, i, prim[h], sp, which, device(h, prim[h], up1(sec[h], by)))

        def two(self, h, k, i, pp, which, by):
            self.put(h, 3 + 3 * k + i, pp, self.order(h, k), which, device(h, up1(prim[h], by), sec[h]))

        def own(self, h, k):
            self.two(h, k, OWN_F, prim[h], "W", 1)
            self.two(h, k, OWN_B, prim[h], "W", 3)

        def wait(self, h, i):
            wait_for(PIECE, ag_recv.at[self.t, h, i])

        def norms(self, sums):
            rows = rows_of(self.t)
            for h in range(2):
                cs = cols_of(h, "W")
                resid[rows, cs] = hid[rows, cs].astype(F32) + sums[h]
            mean = jnp.sum(resid[rows], axis=1, keepdims=True) * (1.0 / WIDTH)
            centered = resid[rows] - mean
            var = jnp.sum(centered * centered, axis=1, keepdims=True) * (1.0 / WIDTH)
            norm[y, z, rows] = (centered * lax.rsqrt(var + EPS) * gain[...] + bias[...]).astype(BF16)

        def start(self):
            for h in range(2):
                self.one(h, OWN_F, sec[h], "W", 1)
                self.one(h, OWN_B, sec[h], "W", 3)
            for h in range(2):
                self.own(h, 0)

        def near(self):
            for h in range(2):
                self.wait(h, OWN_F)
                self.one(h, REL, up1(sec[h], 3), "F", 1)
                self.own(h, 1)
                self.wait(h, OWN_B)
                self.one(h, REL, up1(sec[h], 1), "B", 3)
                self.own(h, 2)

        def far(self):
            for h in range(2):
                self.wait(h, REL)
                self.own(h, 3)

        def relay(self, k):
            for h in range(2):
                self.wait(h, 3 + 3 * k + OWN_F)
                self.two(h, k, REL, up1(prim[h], 3), "F", 1)
                self.wait(h, 3 + 3 * k + OWN_B)
                self.two(h, k, REL, up1(prim[h], 1), "B", 3)

        def done(self, k):
            for h in range(2):
                self.wait(h, 3 + 3 * k + REL)

        def product(self, k):
            rows = rows_of(self.t)
            for h in range(2):
                sp, cs = self.order(h, k), cols_of(h, "W")
                lhs = norm[:, sp, rows, cs] if h == 0 else norm[sp, :, rows, cs]
                value = nt_dot(lhs.reshape(64, HALF), wi[:, cs]).reshape(4, 16, UNITS)
                if h == 0:
                    acc[:, sp, rows] = acc[:, sp, rows] + value
                else:
                    acc[sp, :, rows] = acc[sp, :, rows] + value

        def low_copy(self, i):
            ref = low.at[self.t, m]
            return pltpu.make_async_remote_copy(
                src_ref=ref,
                dst_ref=ref,
                send_sem=low_send.at[self.t],
                recv_sem=low_recv.at[self.t],
                device_id={"mlp": lax.rem(m + i, 16)},
                device_id_type=MESH,
            )

        def inside(self, i):
            lane = lax.broadcasted_iota(jnp.int32, (RANK, 256), 1)
            token = (lane >> 4) * 32 + (lane & 15) + 16 * self.t
            return (token >= starts[i]) & (token < ends[i])

        def lows(self):
            window = pl.ds(pl.multiple_of(lax.div(m * 5 - lax.rem(m, 2), 2) * 128, 128), 384)
            ranks = nt_dot(dsel[...], norm[:, :, rows_of(self.t), window].reshape(256, 384))
            mine = jnp.zeros((RANK, 256), F32)
            for i in range(REQS):
                mine = mine + jnp.where(self.inside(i), ranks[i * RANK : (i + 1) * RANK, :], 0.0)
            low[self.t, m] = mine.astype(BF16)

            def low_start(i, c):
                self.low_copy(i).start()
                return c

            lax.fori_loop(1, 16, low_start, 0)

        def activate(self):
            t, rows = self.t, rows_of(self.t)
            wait_for(low.at[t, 0:15], low_recv.at[t])
            wait_for(low.at[t, 0:15], low_send.at[t])
            lowrank = jnp.sum(low[t].astype(F32), axis=0).astype(BF16).astype(F32)
            for i in range(REQS):
                spread[i * RANK : (i + 1) * RANK, :] = jnp.where(self.inside(i), lowrank, 0.0).astype(BF16)
            for i in range(2):
                adapted = lax.dot_general(
                    spread[:, i * 128 : (i + 1) * 128], usel[...], (((0,), (0,)), ((), ())), preferred_element_type=F32
                )
                two = slice(2 * i, 2 * i + 2)
                preact = acc[two, :, rows] + adapted.reshape(2, 4, 16, UNITS)
                act[two, :, rows] = jax.nn.gelu(preact, approximate=True).astype(BF16)
            for h in range(2):
                wait_for(SENT, ag_send.at[t, h])

    def pages():
        locals_[6].wait()
        locals_[7].wait()
        for t, cache, out in ((1, kc, ko), (2, vc, vo)):
            for page in range(5):
                value = cache[page]
                for b in range(4):
                    value = jnp.where(look[0, b] == page, qkv[t, b * 128 : (b + 1) * 128, :], value)
                out[page] = value

    def pick_down():
        for t, ref in enumerate((downs, ups)):
            wait_for(ref, fac_recv.at[t])
            wait_for(ref.at[0:7], fac_send.at[t])
        picked = jnp.dot(onehot[...], downs[...].reshape(64 * RANK, 320), preferred_element_type=F32)
        dsel_f[...] = jnp.zeros_like(dsel_f)
        dsel_f[:, :320] = picked
        shifted = jnp.where(lax.rem(m, 2) == 1, pltpu.roll(dsel_f[...], 64, 1), dsel_f[...])
        dsel[...] = shifted.astype(BF16)

    def pick_up():
        usel[...] = jnp.dot(onehot[...], ups[...].reshape(64 * RANK, UNITS), preferred_element_type=F32).astype(BF16)

    locals_[0].wait()
    locals_[3].wait()
    a, b = Scatter(0, att, wo), Scatter(1, att, wo)
    c, d = Scatter(0, act, w2), Scatter(1, act, w2)
    ga, gb = Gather(0), Gather(1)
    a.first(0)
    a.first(1)
    b.first(0)
    a.second(0)
    b.first(1)
    a.first(2)
    a.first(3)
    b.second(0)
    a.third(0)
    a.second(1)
    a.second(2)
    b.first(2)
    a.second(3)
    a.third(1)
    a.third(2)
    b.third(0)
    b.second(1)
    b.first(3)
    a.third(3)
    locals_[4].wait()
    locals_[5].wait()
    ga.norms(a.last())
    ga.start()
    b.second(2)
    ga.near()
    b.third(1)
    b.third(2)
    b.second(3)
    ga.far()
    ga.relay(2)
    ga.relay(0)
    pick_down()
    ga.relay(1)
    pick_up()
    b.third(3)
    ga.relay(3)
    gb.norms(b.last())
    gb.start()
    ga.done(2)
    pages()
    ga.done(0)
    locals_[1].wait()
    ga.product(2)
    ga.done(3)
    ga.done(1)
    ga.lows()
    ga.product(3)
    gb.near()
    ga.product(0)
    gb.relay(0)
    ga.product(1)
    ga.activate()
    gb.far()
    locals_[2].wait()
    c.first(0)
    gb.relay(1)
    gb.relay(2)
    gb.done(0)
    gb.product(0)
    gb.relay(3)
    c.first(1)
    c.first(2)
    gb.done(1)
    c.second(0)
    gb.product(1)
    gb.done(2)
    gb.done(3)
    gb.lows()
    c.second(1)
    c.first(3)
    gb.product(3)
    gb.product(2)
    c.third(0)
    c.second(2)
    c.second(3)
    gb.activate()
    d.first(0)
    d.first(1)
    d.first(2)
    d.second(0)
    d.second(1)
    d.first(3)
    d.third(0)
    d.second(2)
    d.second(3)
    c.third(1)
    c.third(2)
    d.third(1)
    c.third(3)
    d.third(2)
    sums = c.last()
    for h in range(2):
        outb[0:16, cols_of(h, "W")] = (resid[0:16, cols_of(h, "W")] + sums[h]).astype(BF16)
    d.third(3)
    sums = d.last()
    for h in range(2):
        outb[16:32, cols_of(h, "W")] = (resid[16:32, cols_of(h, "W")] + sums[h]).astype(BF16)
    wait_for(qkv.at[:, 0:480], a2a_send.at[0])


def shards(*args):
    (queries, keys, values, hidden, w_o, w_in, w_out, gain, bias, down, up, kc, vc, lens, look, adp, slot) = args
    any_, smem = pl.BlockSpec(memory_space=pl.ANY), pl.BlockSpec(memory_space=pltpu.SMEM)
    vmem, dma = pltpu.VMEM, pltpu.SemaphoreType.DMA
    scratch = [
        vmem((3, TOK_G, HEADC), BF16),
        vmem((4, 4, 32, HEADC), BF16),
        vmem((HEADC, WIDTH), BF16),
        vmem((UNITS, WIDTH), BF16),
        vmem((UNITS, WIDTH), BF16),
        vmem((32, WIDTH), BF16),
        vmem((1, WIDTH), F32),
        vmem((1, WIDTH), F32),
        vmem((8, 128, 320), BF16),
        vmem((8, 128, UNITS), BF16),
        vmem((5, 128, HEADC), BF16),
        vmem((5, 128, HEADC), BF16),
        vmem((TOK_G, 1), jnp.int32),
        vmem((4, 4, 32, WIDTH), BF16),
        vmem((4, 4, 32, WIDTH), BF16),
        vmem((2, 4, 32, QUART), BF16),
        vmem((2, 4, 32, QUART), BF16),
        vmem((2, 4, 32, HALF), BF16),
        vmem((2, 4, 32, HALF), BF16),
        vmem((2, 3, 32, HALF), BF16),
        vmem((2, 32, QUART), BF16),
        vmem((2, 32, QUART), BF16),
        vmem((2, 32, HALF), BF16),
        vmem((2, 32, HALF), BF16),
        vmem((32, WIDTH), F32),
        vmem((32, WIDTH), F32),
        vmem((4, 4, 32, UNITS), F32),
        vmem((4, 4, 32, UNITS), BF16),
        vmem((REQS * RANK, 64 * RANK), BF16),
        vmem((REQS * RANK, 384), F32),
        vmem((REQS * RANK, 384), BF16),
        vmem((REQS * RANK, UNITS), BF16),
        vmem((2, 16, RANK, 256), BF16),
        vmem((REQS * RANK, 256), BF16),
        dma((8,)),
        dma((1,)),
        dma((2,)),
        dma((2,)),
        dma((2,)),
        dma((2,)),
        dma((2,)),
        dma((2, 2)),
        dma((2, 2, 15)),
        dma((2, 2)),
        dma((2, 2, 15)),
    ]
    return pl.pallas_call(
        kernel,
        out_shape=(
            pltpu.VMEM((32, WIDTH), BF16),
            pltpu.VMEM((5, 128, HEADC), BF16),
            pltpu.VMEM((5, 128, HEADC), BF16),
        ),
        in_specs=[any_] * 13 + [smem] * 4,
        out_specs=(pl.BlockSpec(memory_space=pltpu.VMEM),) * 3,
        scratch_shapes=scratch,
        compiler_params=pltpu.CompilerParams(
            collective_id=0, has_side_effects=True, vmem_limit_bytes=62 * 1024 * 1024
        ),
    )(
        queries, keys, values, hidden, w_o, w_in.T, w_out, gain.reshape(1, WIDTH), bias.reshape(1, WIDTH),
        jnp.transpose(down, (0, 2, 1)).reshape(128, 320), up.reshape(128, UNITS), kc, vc, lens, look, adp, slot,
    )


def solution(mesh):
    in_specs = (
        P(("req", "mlp"), None),
        P(("req", "mlp"), None),
        P(("req", "mlp"), None),
        P(("req", "mlp"), None),
        P("mlp", None),
        P(None, "mlp"),
        P("mlp", None),
        P(),
        P(),
        P("req", "mlp", None),
        P("req", None, "mlp"),
        P("req", None, "mlp"),
        P("req", None, "mlp"),
        P("req", None),
        P("req", None),
        P("req", None),
        P(),
    )
    out_specs = (P(("req", "mlp"), None), P("req", None, "mlp"), P("req", None, "mlp"))
    return jax.shard_map(shards, mesh=mesh, in_specs=in_specs, out_specs=out_specs, check_vma=False)
```

```python
import functools

import jax
import jax.numpy as jnp
from jax import lax
from jax.experimental import pallas as pl
from jax.experimental.pallas import tpu as pltpu
from jax.sharding import PartitionSpec as P

MESH = pl.DeviceIdType.MESH
HS = 128
RANK = 16
REQS = 16
TOK_G = 512
WIDTH = 5120
HALF = WIDTH // 2
QUART = HALF // 2
UNITS = 864
HEADC = 256
TILE = 512
EPS = 1e-06
F32 = jnp.float32
BF16 = jnp.bfloat16

RELAY, FULL = range(2)
R2F, R2B, FULL2 = range(8, 11)
OWN, REL = range(2)


def nt_dot(a, b):
    return lax.dot_general(a, b, (((1,), (1,)), ((), ())), preferred_element_type=F32)


def kernel(
    q_hbm, k_hbm, v_hbm, hid_hbm, wo_hbm, wi_hbm, w2_hbm, gain_hbm, bias_hbm, down_hbm, up_hbm, kc_hbm, vc_hbm,
    lens, look, adp, slot,
    outb, ko, vo,
    qkv, att, wo, wi, w2, hid, gain, bias, downs, ups, kc, vc, start_col,
    part, norm, relay_f, relay_b, full_f, full_b, mid, relay2_f, relay2_b, full2_f, full2_b,
    resid, total, acc, act, onehot, dsel_f, dsel, usel, low, spread,
    local_sem, a2a_send, a2a_recv, fac_send, fac_recv, low_send, low_recv, rs_send, rs_recv, ag_send, ag_recv,
):
    m = lax.axis_index("mlp")
    r = lax.axis_index("req")
    y, z = lax.div(m, 4), lax.rem(m, 4)

    def place(h, p, s):
        return (p, s) if h == 0 else (s, p)

    def device(h, p, s):
        a, b = place(h, p, s)
        return {"mlp": a * 4 + b}

    prim = (y, z)
    sec = (z, y)

    def up1(i, by):
        return lax.rem(i + by, 4)

    def wait_for(like, sem):
        pltpu.make_async_copy(like, like, sem).wait()

    locals_ = {}

    def local(i, src, dst):
        c = pltpu.make_async_copy(src, dst, local_sem.at[i])
        c.start()
        locals_[i] = c

    local(0, wo_hbm, wo)
    local(3, hid_hbm, hid)
    local(4, gain_hbm, gain)
    local(5, bias_hbm, bias)
    local(6, kc_hbm, kc)
    local(7, vc_hbm, vc)
    pltpu.make_async_copy(down_hbm, downs.at[r], fac_recv.at[0]).start()
    pltpu.make_async_copy(up_hbm, ups.at[r], fac_recv.at[1]).start()
    own_rows = pl.ds(pl.multiple_of(m * 32, 32), 32)
    for h in range(2):
        for t, ref in enumerate((q_hbm, k_hbm, v_hbm)):
            cols = pl.ds(pl.multiple_of(m * HEADC + h * HS, HS), HS)
            mine = qkv.at[t, own_rows, h * HS : (h + 1) * HS]
            pltpu.make_async_copy(ref.at[:, cols], mine, a2a_recv.at[h]).start()

    barrier = pltpu.get_barrier_semaphore()

    def greet_mlp(i, c):
        pl.semaphore_signal(barrier, inc=1, device_id={"mlp": lax.rem(m + i, 16)}, device_id_type=MESH)
        return c

    def greet_req(i, c):
        pl.semaphore_signal(barrier, inc=1, device_id={"req": lax.rem(r + i, 8)}, device_id_type=MESH)
        return c

    lax.fori_loop(1, 16, greet_mlp, 0)
    lax.fori_loop(1, 8, greet_req, 0)
    pl.semaphore_wait(barrier, 22)

    def a2a_copy(h, t, ref, i):
        d = lax.rem(m + i, 16)
        return pltpu.make_async_remote_copy(
            src_ref=ref.at[:, pl.ds(pl.multiple_of(d * HEADC + h * HS, HS), HS)],
            dst_ref=qkv.at[t, own_rows, h * HS : (h + 1) * HS],
            send_sem=a2a_send.at[0],
            recv_sem=a2a_recv.at[h],
            device_id={"mlp": d},
            device_id_type=MESH,
        )

    for h in range(2):

        def a2a_start(i, c, h=h):
            for t, ref in enumerate((q_hbm, k_hbm, v_hbm)):
                a2a_copy(h, t, ref, i).start()
            return c

        lax.fori_loop(1, 16, a2a_start, 0)

    def fac_copy(t, src, dst, i):
        return pltpu.make_async_remote_copy(
            src_ref=src,
            dst_ref=dst.at[r],
            send_sem=fac_send.at[t],
            recv_sem=fac_recv.at[t],
            device_id={"req": lax.rem(r + i, 8)},
            device_id_type=MESH,
        )

    def fac_start(i, c):
        fac_copy(0, down_hbm, downs, i).start()
        fac_copy(1, up_hbm, ups, i).start()
        return c

    lax.fori_loop(1, 8, fac_start, 0)
    local(1, wi_hbm, wi)
    local(2, w2_hbm, w2)

    pos = lax.broadcasted_iota(jnp.int32, (TOK_G, 1), 0)
    starts, ends = [], []
    first = jnp.zeros((TOK_G, 1), jnp.int32)
    end = jnp.int32(0)
    for i in range(REQS):
        starts.append(end)
        end = end + lens[0, i]
        ends.append(end)
        first = jnp.where(pos >= end, end, first)
    start_col[...] = first

    for i in range(REQS):
        wanted = slot[adp[0, i]] * RANK
        lane = lax.broadcasted_iota(jnp.int32, (RANK, 64 * RANK), 1)
        sub = lax.broadcasted_iota(jnp.int32, (RANK, 64 * RANK), 0)
        onehot[i * RANK : (i + 1) * RANK, :] = (lane - sub == wanted).astype(F32).astype(BF16)
    acc[...] = jnp.zeros_like(acc)


    for h in range(2):
        hc = slice(h * HS, (h + 1) * HS)
        wait_for(qkv.at[:, :, hc], a2a_recv.at[h])
        for i in range(4):
            rows, length = slice(i * 128, (i + 1) * 128), (i + 1) * 128
            score = nt_dot(qkv[0, rows, hc], qkv[1, :length, hc]) * (HS ** (-0.5))
            qi = lax.broadcasted_iota(jnp.int32, (128, length), 0) + i * 128
            kj = lax.broadcasted_iota(jnp.int32, (128, length), 1)
            allowed = (kj <= qi) & (kj >= start_col[rows, :])
            score = jnp.where(allowed, score, -1e30)
            expo = jnp.exp(score - jnp.max(score, axis=1, keepdims=True))
            weights = (expo / jnp.sum(expo, axis=1, keepdims=True)).astype(BF16)
            mixed = jnp.dot(weights, qkv[2, :length, hc], preferred_element_type=F32)
            att[i, :, :, hc] = mixed.astype(BF16).reshape(4, 32, HS)

    def remote(src, dst, sems, t, h, i, dev):
        c = pltpu.make_async_remote_copy(
            src_ref=src,
            dst_ref=dst,
            send_sem=sems[0].at[t, h],
            recv_sem=sems[1].at[t, h, i],
            device_id=dev,
            device_id_type=MESH,
        )
        c.start()

    def rows_of(t):
        return slice(16 * t, 16 * t + 16)

    def cols_of(h, which):
        base = h * HALF
        if which == "F":
            return slice(base, base + QUART)
        if which == "B":
            return slice(base + QUART, base + HALF)
        return slice(base, base + HALF)

    UNIT, PIECE, PAIR, SENT = wo.at[0:16, :QUART], wo.at[0:16, :HALF], wo.at[0:16], wo.at[0:240, :HALF]

    class Scatter:
        def __init__(self, t, left, right):
            self.t, self.left, self.right = t, left, right
            self.sems = (rs_send, rs_recv)

        def at(self, h, p, s, which):
            a, b = place(h, p, s)
            return (a, b, rows_of(self.t), cols_of(h, which))

        def order(self, h, k):
            return up1(sec[h], (2, 1, 3, 0)[k])

        def product(self, h, k):
            s, rows = self.order(h, k), rows_of(self.t)
            left, right = self.left, self.right
            lhs = left[:, s, rows] if h == 0 else left[s, :, rows]
            lhs = lhs.reshape(64, left.shape[3])
            for c in range(h * HALF, (h + 1) * HALF, TILE):
                value = jnp.dot(lhs, right[:, c : c + TILE], preferred_element_type=F32).astype(BF16)
                value = value.reshape(4, 16, TILE)
                if h == 0:
                    part[:, s, rows, c : c + TILE] = value
                else:
                    part[s, :, rows, c : c + TILE] = value

        def first(self, k, h):
            t, rows, sems = self.t, rows_of(self.t), self.sems
            self.product(h, k)
            p, s, sp = prim[h], sec[h], self.order(h, k)
            ahead, behind = device(h, up1(p, 1), s), device(h, up1(p, 3), s)
            far, i = up1(p, 2), 2 * k
            remote(part.at[self.at(h, far, sp, "F")], relay_f.at[h, k, rows], sems, t, h, i + RELAY, ahead)
            remote(part.at[self.at(h, far, sp, "B")], relay_b.at[h, k, rows], sems, t, h, i + RELAY, behind)
            remote(part.at[self.at(h, up1(p, 1), sp, "B")], full_f.at[h, k, rows, QUART:], sems, t, h, i + FULL, ahead)
            remote(part.at[self.at(h, up1(p, 3), sp, "F")], full_b.at[h, k, rows, :QUART], sems, t, h, i + FULL, behind)

        def second(self, k):
            t, rows, sems = self.t, rows_of(self.t), self.sems
            for h in range(2):
                p, s, sp = prim[h], sec[h], self.order(h, k)
                ahead, behind = device(h, up1(p, 1), s), device(h, up1(p, 3), s)
                i = 2 * k
                wait_for(PIECE, rs_recv.at[t, h, i + RELAY])
                at = self.at(h, up1(p, 1), sp, "F")
                part[at] = (part[at].astype(F32) + relay_f[h, k, rows].astype(F32)).astype(BF16)
                remote(part.at[at], full_f.at[h, k, rows, :QUART], sems, t, h, i + FULL, ahead)
                at = self.at(h, up1(p, 3), sp, "B")
                part[at] = (part[at].astype(F32) + relay_b[h, k, rows].astype(F32)).astype(BF16)
                remote(part.at[at], full_b.at[h, k, rows, QUART:], sems, t, h, i + FULL, behind)

        def third(self, k):
            t, rows, sems = self.t, rows_of(self.t), self.sems
            for h in range(2):
                p, s, sp = prim[h], sec[h], self.order(h, k)
                wait_for(PAIR, rs_recv.at[t, h, 2 * k + FULL])
                value = (
                    part[self.at(h, p, sp, "W")].astype(F32)
                    + full_f[h, k, rows].astype(F32)
                    + full_b[h, k, rows].astype(F32)
                )
                ahead, behind = device(h, p, up1(s, 1)), device(h, p, up1(s, 3))
                if k == 0:
                    mid[h, 0, rows] = value.astype(BF16)
                    remote(mid.at[h, 0, rows, :QUART], relay2_f.at[h, rows], sems, t, h, R2F, ahead)
                    remote(mid.at[h, 0, rows, QUART:], relay2_b.at[h, rows], sems, t, h, R2B, behind)
                elif k == 1:
                    wait_for(UNIT, rs_recv.at[t, h, R2F])
                    mid[h, 1, rows, :QUART] = (value[:, :QUART] + relay2_f[h, rows].astype(F32)).astype(BF16)
                    mid[h, 1, rows, QUART:] = value[:, QUART:].astype(BF16)
                    remote(mid.at[h, 1, rows], full2_f.at[h, rows], sems, t, h, FULL2, ahead)
                elif k == 2:
                    wait_for(UNIT, rs_recv.at[t, h, R2B])
                    mid[h, 2, rows, :QUART] = value[:, :QUART].astype(BF16)
                    mid[h, 2, rows, QUART:] = (value[:, QUART:] + relay2_b[h, rows].astype(F32)).astype(BF16)
                    remote(mid.at[h, 2, rows], full2_b.at[h, rows], sems, t, h, FULL2, behind)
                else:
                    total[rows, cols_of(h, "W")] = value

        def last(self):
            rows = rows_of(self.t)
            for h in range(2):
                wait_for(PAIR, rs_recv.at[self.t, h, FULL2])
                wait_for(SENT, rs_send.at[self.t, h])
            return [
                total[rows, cols_of(h, "W")] + full2_f[h, rows].astype(F32) + full2_b[h, rows].astype(F32)
                for h in range(2)
            ]

    class Gather:
        def __init__(self, t):
            self.t = t
            self.sems = (ag_send, ag_recv)

        def order(self, h, k):
            return up1(sec[h], (0, 3, 1, 2)[k])

        def put(self, h, i, pp, sp, which, dev):
            a, b = place(h, pp, sp)
            ref = norm.at[a, b, rows_of(self.t), cols_of(h, which)]
            remote(ref, ref, self.sems, self.t, h, i, dev)

        def one(self, h, i, sp, which, by):
            self.put(h, i, prim[h], sp, which, device(h, prim[h], up1(sec[h], by)))

        def two(self, h, k, i, pp, which, by):
            self.put(h, 2 + 2 * k + i, pp, self.order(h, k), which, device(h, up1(prim[h], by), sec[h]))

        def own(self, h, k):
            self.two(h, k, OWN, prim[h], "W", 1)
            self.two(h, k, OWN, prim[h], "W", 3)

        def wait(self, h, i):
            wait_for(PAIR if i % 2 == OWN else PIECE, ag_recv.at[self.t, h, i])

        def norms(self, sums):
            rows = rows_of(self.t)
            for h in range(2):
                cs = cols_of(h, "W")
                resid[rows, cs] = hid[rows, cs].astype(F32) + sums[h]
            mean = jnp.sum(resid[rows], axis=1, keepdims=True) * (1.0 / WIDTH)
            centered = resid[rows] - mean
            var = jnp.sum(centered * centered, axis=1, keepdims=True) * (1.0 / WIDTH)
            norm[y, z, rows] = (centered * lax.rsqrt(var + EPS) * gain[...] + bias[...]).astype(BF16)

        def start(self):
            for h in range(2):
                self.one(h, OWN, sec[h], "W", 1)
                self.one(h, OWN, sec[h], "W", 3)
            for h in range(2):
                self.own(h, 0)

        def near(self):
            for h in range(2):
                self.wait(h, OWN)
                self.one(h, REL, up1(sec[h], 3), "F", 1)
                self.own(h, 1)
                self.one(h, REL, up1(sec[h], 1), "B", 3)
                self.own(h, 2)

        def far(self):
            for h in range(2):
                self.wait(h, REL)
                self.own(h, 3)

        def relay(self, k):
            for h in range(2):
                self.wait(h, 2 + 2 * k + OWN)
                self.two(h, k, REL, up1(prim[h], 3), "F", 1)
                self.two(h, k, REL, up1(prim[h], 1), "B", 3)

        def done(self, k):
            for h in range(2):
                self.wait(h, 2 + 2 * k + REL)

        def product(self, k, h):
            rows = rows_of(self.t)
            sp, cs = self.order(h, k), cols_of(h, "W")
            lhs = norm[:, sp, rows, cs] if h == 0 else norm[sp, :, rows, cs]
            value = nt_dot(lhs.reshape(64, HALF), wi[:, cs]).reshape(4, 16, UNITS)
            if h == 0:
                acc[:, sp, rows] = acc[:, sp, rows] + value
            else:
                acc[sp, :, rows] = acc[sp, :, rows] + value

        def low_copy(self, i):
            ref = low.at[self.t, m]
            return pltpu.make_async_remote_copy(
                src_ref=ref,
                dst_ref=ref,
                send_sem=low_send.at[self.t],
                recv_sem=low_recv.at[self.t],
                device_id={"mlp": lax.rem(m + i, 16)},
                device_id_type=MESH,
            )

        def inside(self, i):
            lane = lax.broadcasted_iota(jnp.int32, (RANK, 256), 1)
            token = (lane >> 4) * 32 + (lane & 15) + 16 * self.t
            return (token >= starts[i]) & (token < ends[i])

        def lows(self):
            window = pl.ds(pl.multiple_of(lax.div(m * 5 - lax.rem(m, 2), 2) * 128, 128), 384)
            ranks = nt_dot(dsel[...], norm[:, :, rows_of(self.t), window].reshape(256, 384))
            mine = jnp.zeros((RANK, 256), F32)
            for i in range(REQS):
                mine = mine + jnp.where(self.inside(i), ranks[i * RANK : (i + 1) * RANK, :], 0.0)
            low[self.t, m] = mine.astype(BF16)

            def low_start(i, c):
                self.low_copy(i).start()
                return c

            lax.fori_loop(1, 16, low_start, 0)

        def activate(self):
            t, rows = self.t, rows_of(self.t)
            wait_for(low.at[t, 0:15], low_recv.at[t])
            wait_for(low.at[t, 0:15], low_send.at[t])
            lowrank = jnp.sum(low[t].astype(F32), axis=0).astype(BF16).astype(F32)
            for i in range(REQS):
                spread[i * RANK : (i + 1) * RANK, :] = jnp.where(self.inside(i), lowrank, 0.0).astype(BF16)
            for i in range(2):
                adapted = lax.dot_general(
                    spread[:, i * 128 : (i + 1) * 128], usel[...], (((0,), (0,)), ((), ())), preferred_element_type=F32
                )
                two = slice(2 * i, 2 * i + 2)
                preact = acc[two, :, rows] + adapted.reshape(2, 4, 16, UNITS)
                act[two, :, rows] = jax.nn.gelu(preact, approximate=True).astype(BF16)
            for h in range(2):
                wait_for(SENT, ag_send.at[t, h])

    def pages():
        locals_[6].wait()
        locals_[7].wait()
        for t, cache, out in ((1, kc, ko), (2, vc, vo)):
            for page in range(5):
                value = cache[page]
                for b in range(4):
                    value = jnp.where(look[0, b] == page, qkv[t, b * 128 : (b + 1) * 128, :], value)
                out[page] = value

    def pick_down():
        for t, ref in enumerate((downs, ups)):
            wait_for(ref, fac_recv.at[t])
            wait_for(ref.at[0:7], fac_send.at[t])
        picked = jnp.dot(onehot[...], downs[...].reshape(64 * RANK, 320), preferred_element_type=F32)
        dsel_f[...] = jnp.zeros_like(dsel_f)
        dsel_f[:, :320] = picked
        shifted = jnp.where(lax.rem(m, 2) == 1, pltpu.roll(dsel_f[...], 64, 1), dsel_f[...])
        dsel[...] = shifted.astype(BF16)

    def pick_up():
        usel[...] = jnp.dot(onehot[...], ups[...].reshape(64 * RANK, UNITS), preferred_element_type=F32).astype(BF16)

    locals_[0].wait()
    locals_[3].wait()
    a, b = Scatter(0, att, wo), Scatter(1, att, wo)
    c, d = Scatter(0, act, w2), Scatter(1, act, w2)
    ga, gb = Gather(0), Gather(1)
    a.first(0, 0)
    a.first(0, 1)
    a.first(1, 0)
    a.first(1, 1)
    b.first(0, 0)
    b.first(0, 1)
    a.second(0)
    b.first(1, 0)
    b.first(1, 1)
    a.first(2, 0)
    a.first(2, 1)
    a.first(3, 0)
    a.first(3, 1)
    b.second(0)
    a.third(0)
    a.second(1)
    a.second(2)
    b.first(2, 0)
    b.first(2, 1)
    a.second(3)
    a.third(1)
    a.third(2)
    b.third(0)
    b.second(1)
    b.first(3, 0)
    b.first(3, 1)
    a.third(3)
    locals_[4].wait()
    locals_[5].wait()
    ga.norms(a.last())
    ga.start()
    b.second(2)
    ga.near()
    b.third(1)
    b.third(2)
    b.second(3)
    ga.far()
    ga.relay(2)
    ga.relay(0)
    pick_down()
    ga.relay(1)
    pick_up()
    b.third(3)
    ga.relay(3)
    gb.norms(b.last())
    gb.start()
    ga.done(2)
    pages()
    ga.done(0)
    locals_[1].wait()
    ga.product(2, 0)
    ga.product(2, 1)
    ga.done(3)
    ga.done(1)
    ga.lows()
    ga.product(3, 0)
    ga.product(3, 1)
    gb.near()
    ga.product(0, 0)
    ga.product(0, 1)
    gb.relay(0)
    ga.product(1, 0)
    ga.product(1, 1)
    ga.activate()
    gb.far()
    locals_[2].wait()
    c.first(0, 0)
    c.first(0, 1)
    gb.relay(1)
    gb.relay(2)
    gb.done(0)
    gb.product(0, 0)
    gb.product(0, 1)
    gb.relay(3)
    c.first(1, 0)
    c.first(1, 1)
    c.first(2, 0)
    c.first(2, 1)
    gb.done(1)
    c.second(0)
    gb.product(1, 0)
    gb.product(1, 1)
    gb.done(2)
    gb.done(3)
    gb.lows()
    c.second(1)
    c.first(3, 0)
    c.first(3, 1)
    gb.product(3, 0)
    gb.product(3, 1)
    gb.product(2, 0)
    gb.product(2, 1)
    c.third(0)
    c.second(2)
    c.second(3)
    gb.activate()
    d.first(0, 0)
    d.first(0, 1)
    d.first(1, 0)
    d.first(1, 1)
    d.first(2, 0)
    d.first(2, 1)
    d.second(0)
    d.second(1)
    d.first(3, 0)
    d.first(3, 1)
    d.third(0)
    d.second(2)
    d.second(3)
    c.third(1)
    c.third(2)
    d.third(1)
    c.third(3)
    d.third(2)
    sums = c.last()
    for h in range(2):
        outb[0:16, cols_of(h, "W")] = (resid[0:16, cols_of(h, "W")] + sums[h]).astype(BF16)
    d.third(3)
    sums = d.last()
    for h in range(2):
        outb[16:32, cols_of(h, "W")] = (resid[16:32, cols_of(h, "W")] + sums[h]).astype(BF16)
    wait_for(qkv.at[:, 0:480], a2a_send.at[0])


def writer(a, b, c, to_a, to_b, to_c, sem):
    copies = [pltpu.make_async_copy(x, o, sem.at[i]) for i, (x, o) in enumerate(((a, to_a), (b, to_b), (c, to_c)))]
    for copy in copies:
        copy.start()
    for copy in copies:
        copy.wait()


def written(results):
    any_ = pl.BlockSpec(memory_space=pl.ANY)
    return pl.pallas_call(
        writer,
        out_shape=tuple(jax.ShapeDtypeStruct(v.shape, v.dtype) for v in results),
        in_specs=[pl.BlockSpec(memory_space=pltpu.VMEM)] * 3,
        out_specs=(any_,) * 3,
        scratch_shapes=[pltpu.SemaphoreType.DMA((3,))],
    )(*(pltpu.with_memory_space_constraint(v, pltpu.VMEM) for v in results))


def shards(*args):
    (queries, keys, values, hidden, w_o, w_in, w_out, gain, bias, down, up, kc, vc, lens, look, adp, slot) = args
    any_, smem = pl.BlockSpec(memory_space=pl.ANY), pl.BlockSpec(memory_space=pltpu.SMEM)
    vmem, dma = pltpu.VMEM, pltpu.SemaphoreType.DMA
    scratch = [
        vmem((3, TOK_G, HEADC), BF16),
        vmem((4, 4, 32, HEADC), BF16),
        vmem((HEADC, WIDTH), BF16),
        vmem((UNITS, WIDTH), BF16),
        vmem((UNITS, WIDTH), BF16),
        vmem((32, WIDTH), BF16),
        vmem((1, WIDTH), F32),
        vmem((1, WIDTH), F32),
        vmem((8, 128, 320), BF16),
        vmem((8, 128, UNITS), BF16),
        vmem((5, 128, HEADC), BF16),
        vmem((5, 128, HEADC), BF16),
        vmem((TOK_G, 1), jnp.int32),
        vmem((4, 4, 32, WIDTH), BF16),
        vmem((4, 4, 32, WIDTH), BF16),
        vmem((2, 4, 32, QUART), BF16),
        vmem((2, 4, 32, QUART), BF16),
        vmem((2, 4, 32, HALF), BF16),
        vmem((2, 4, 32, HALF), BF16),
        vmem((2, 3, 32, HALF), BF16),
        vmem((2, 32, QUART), BF16),
        vmem((2, 32, QUART), BF16),
        vmem((2, 32, HALF), BF16),
        vmem((2, 32, HALF), BF16),
        vmem((32, WIDTH), F32),
        vmem((32, WIDTH), F32),
        vmem((4, 4, 32, UNITS), F32),
        vmem((4, 4, 32, UNITS), BF16),
        vmem((REQS * RANK, 64 * RANK), BF16),
        vmem((REQS * RANK, 384), F32),
        vmem((REQS * RANK, 384), BF16),
        vmem((REQS * RANK, UNITS), BF16),
        vmem((2, 16, RANK, 256), BF16),
        vmem((REQS * RANK, 256), BF16),
        dma((8,)),
        dma((1,)),
        dma((2,)),
        dma((2,)),
        dma((2,)),
        dma((2,)),
        dma((2,)),
        dma((2, 2)),
        dma((2, 2, 11)),
        dma((2, 2)),
        dma((2, 2, 10)),
    ]
    results = pl.pallas_call(
        kernel,
        out_shape=(
            pltpu.VMEM((32, WIDTH), BF16),
            pltpu.VMEM((5, 128, HEADC), BF16),
            pltpu.VMEM((5, 128, HEADC), BF16),
        ),
        in_specs=[any_] * 13 + [smem] * 4,
        out_specs=(pl.BlockSpec(memory_space=pltpu.VMEM),) * 3,
        scratch_shapes=scratch,
        compiler_params=pltpu.CompilerParams(
            collective_id=0, has_side_effects=True, vmem_limit_bytes=62 * 1024 * 1024
        ),
    )(
        queries, keys, values, hidden, w_o, w_in.T, w_out, gain.reshape(1, WIDTH), bias.reshape(1, WIDTH),
        jnp.transpose(down, (0, 2, 1)).reshape(128, 320), up.reshape(128, UNITS), kc, vc, lens, look, adp, slot,
    )
    return written(results)


def solution(mesh):
    in_specs = (
        P(("req", "mlp"), None),
        P(("req", "mlp"), None),
        P(("req", "mlp"), None),
        P(("req", "mlp"), None),
        P("mlp", None),
        P(None, "mlp"),
        P("mlp", None),
        P(),
        P(),
        P("req", "mlp", None),
        P("req", None, "mlp"),
        P("req", None, "mlp"),
        P("req", None, "mlp"),
        P("req", None),
        P("req", None),
        P("req", None),
        P(),
    )
    out_specs = (P(("req", "mlp"), None), P("req", None, "mlp"), P("req", None, "mlp"))
    return jax.shard_map(shards, mesh=mesh, in_specs=in_specs, out_specs=out_specs, check_vma=False)
```

```python
import functools

import jax
import jax.numpy as jnp
from jax import lax
from jax.experimental import pallas as pl
from jax.experimental.pallas import tpu as pltpu
from jax.sharding import PartitionSpec as P

MESH = pl.DeviceIdType.MESH
HS = 128
RANK = 16
REQS = 16
TOK_G = 512
WIDTH = 5120
HALF = WIDTH // 2
QUART = HALF // 2
UNITS = 864
HEADC = 256
TILE = 512
EPS = 1e-06
F32 = jnp.float32
BF16 = jnp.bfloat16

RELAY, FULL = range(2)
R2F, R2B, FULL2 = range(8, 11)
OWN, REL = range(2)


def nt_dot(a, b):
    return lax.dot_general(a, b, (((1,), (1,)), ((), ())), preferred_element_type=F32)


def kernel(
    q_hbm, k_hbm, v_hbm, hid_hbm, wo_hbm, wi_hbm, w2_hbm, gain_hbm, bias_hbm, down_hbm, up_hbm, kc_hbm, vc_hbm,
    lens, look, adp, slot,
    outb, ko, vo,
    qkv, att, wo, wi, w2, hid, gain, bias, downs, ups, kc, vc, start_col,
    part, norm, relay_f, relay_b, full_f, full_b, mid, relay2_f, relay2_b, full2_f, full2_b,
    resid, total, acc, act, onehot, dsel_f, dsel, usel, low, spread,
    local_sem, a2a_send, a2a_recv, fac_send, fac_recv, low_send, low_recv, rs_send, rs_recv, ag_send, ag_recv,
):
    m = lax.axis_index("mlp")
    r = lax.axis_index("req")
    y, z = lax.div(m, 4), lax.rem(m, 4)

    def place(h, p, s):
        return (p, s) if h == 0 else (s, p)

    def device(h, p, s):
        a, b = place(h, p, s)
        return {"mlp": a * 4 + b}

    prim = (y, z)
    sec = (z, y)

    def up1(i, by):
        return lax.rem(i + by, 4)

    def wait_for(like, sem):
        pltpu.make_async_copy(like, like, sem).wait()

    locals_ = {}

    def local(i, src, dst):
        c = pltpu.make_async_copy(src, dst, local_sem.at[i])
        c.start()
        locals_[i] = c

    local(0, wo_hbm, wo)
    local(3, hid_hbm, hid)
    local(4, gain_hbm, gain)
    local(5, bias_hbm, bias)
    local(6, kc_hbm, kc)
    local(7, vc_hbm, vc)
    pltpu.make_async_copy(down_hbm, downs.at[r], fac_recv.at[0]).start()
    pltpu.make_async_copy(up_hbm, ups.at[r], fac_recv.at[1]).start()
    own_rows = pl.ds(pl.multiple_of(m * 32, 32), 32)
    for h in range(2):
        for t, ref in enumerate((q_hbm, k_hbm, v_hbm)):
            cols = pl.ds(pl.multiple_of(m * HEADC + h * HS, HS), HS)
            mine = qkv.at[t, own_rows, h * HS : (h + 1) * HS]
            pltpu.make_async_copy(ref.at[:, cols], mine, a2a_recv.at[h]).start()

    barrier = pltpu.get_barrier_semaphore()

    def greet_mlp(i, c):
        pl.semaphore_signal(barrier, inc=1, device_id={"mlp": lax.rem(m + i, 16)}, device_id_type=MESH)
        return c

    def greet_req(i, c):
        pl.semaphore_signal(barrier, inc=1, device_id={"req": lax.rem(r + i, 8)}, device_id_type=MESH)
        return c

    lax.fori_loop(1, 16, greet_mlp, 0)
    lax.fori_loop(1, 8, greet_req, 0)
    pl.semaphore_wait(barrier, 22)

    def far_first(i):
        return lax.rem(2 + 3 * i + 3 * lax.div(i * (i - 1), 2), 4)

    def a2a_copy(h, t, ref, i):
        d = up1(y, far_first(lax.div(i, 4))) * 4 + up1(z, far_first(lax.rem(i, 4)))
        return pltpu.make_async_remote_copy(
            src_ref=ref.at[:, pl.ds(pl.multiple_of(d * HEADC + h * HS, HS), HS)],
            dst_ref=qkv.at[t, own_rows, h * HS : (h + 1) * HS],
            send_sem=a2a_send.at[0],
            recv_sem=a2a_recv.at[h],
            device_id={"mlp": d},
            device_id_type=MESH,
        )

    for h in range(2):

        def a2a_start(i, c, h=h):
            for t, ref in enumerate((q_hbm, k_hbm, v_hbm)):
                a2a_copy(h, t, ref, i).start()
            return c

        lax.fori_loop(0, 15, a2a_start, 0)

    def fac_copy(t, src, dst, i):
        return pltpu.make_async_remote_copy(
            src_ref=src,
            dst_ref=dst.at[r],
            send_sem=fac_send.at[t],
            recv_sem=fac_recv.at[t],
            device_id={"req": lax.rem(r + i, 8)},
            device_id_type=MESH,
        )

    def fac_start(i, c):
        fac_copy(0, down_hbm, downs, i).start()
        fac_copy(1, up_hbm, ups, i).start()
        return c

    lax.fori_loop(1, 8, fac_start, 0)
    local(1, wi_hbm, wi)
    local(2, w2_hbm, w2)

    pos = lax.broadcasted_iota(jnp.int32, (TOK_G, 1), 0)
    starts, ends = [], []
    first = jnp.zeros((TOK_G, 1), jnp.int32)
    end = jnp.int32(0)
    for i in range(REQS):
        starts.append(end)
        end = end + lens[0, i]
        ends.append(end)
        first = jnp.where(pos >= end, end, first)
    start_col[...] = first

    for i in range(REQS):
        wanted = slot[adp[0, i]] * RANK
        lane = lax.broadcasted_iota(jnp.int32, (RANK, 64 * RANK), 1)
        sub = lax.broadcasted_iota(jnp.int32, (RANK, 64 * RANK), 0)
        onehot[i * RANK : (i + 1) * RANK, :] = (lane - sub == wanted).astype(F32).astype(BF16)
    acc[...] = jnp.zeros_like(acc)


    for h in range(2):
        hc = slice(h * HS, (h + 1) * HS)
        wait_for(qkv.at[:, :, hc], a2a_recv.at[h])
        for i in range(4):
            rows, length = slice(i * 128, (i + 1) * 128), (i + 1) * 128
            score = nt_dot(qkv[0, rows, hc], qkv[1, :length, hc]) * (HS ** (-0.5))
            qi = lax.broadcasted_iota(jnp.int32, (128, length), 0) + i * 128
            kj = lax.broadcasted_iota(jnp.int32, (128, length), 1)
            allowed = (kj <= qi) & (kj >= start_col[rows, :])
            score = jnp.where(allowed, score, -1e30)
            expo = jnp.exp(score - jnp.max(score, axis=1, keepdims=True))
            weights = (expo / jnp.sum(expo, axis=1, keepdims=True)).astype(BF16)
            mixed = jnp.dot(weights, qkv[2, :length, hc], preferred_element_type=F32)
            att[i, :, :, hc] = mixed.astype(BF16).reshape(4, 32, HS)

    def remote(src, dst, sems, t, h, i, dev):
        c = pltpu.make_async_remote_copy(
            src_ref=src,
            dst_ref=dst,
            send_sem=sems[0].at[t, h],
            recv_sem=sems[1].at[t, h, i],
            device_id=dev,
            device_id_type=MESH,
        )
        c.start()

    def rows_of(t):
        return slice(16 * t, 16 * t + 16)

    def cols_of(h, which):
        base = h * HALF
        if which == "F":
            return slice(base, base + QUART)
        if which == "B":
            return slice(base + QUART, base + HALF)
        return slice(base, base + HALF)

    UNIT, PIECE, PAIR, SENT = wo.at[0:16, :QUART], wo.at[0:16, :HALF], wo.at[0:16], wo.at[0:240, :HALF]

    class Scatter:
        def __init__(self, t, left, right):
            self.t, self.left, self.right = t, left, right
            self.sems = (rs_send, rs_recv)

        def at(self, h, p, s, which):
            a, b = place(h, p, s)
            return (a, b, rows_of(self.t), cols_of(h, which))

        def order(self, h, k):
            return up1(sec[h], (2, 1, 3, 0)[k])

        def product(self, h, k):
            s, rows = self.order(h, k), rows_of(self.t)
            left, right = self.left, self.right
            lhs = left[:, s, rows] if h == 0 else left[s, :, rows]
            lhs = lhs.reshape(64, left.shape[3])
            for c in range(h * HALF, (h + 1) * HALF, TILE):
                value = jnp.dot(lhs, right[:, c : c + TILE], preferred_element_type=F32).astype(BF16)
                value = value.reshape(4, 16, TILE)
                if h == 0:
                    part[:, s, rows, c : c + TILE] = value
                else:
                    part[s, :, rows, c : c + TILE] = value

        def first(self, k, h):
            t, rows, sems = self.t, rows_of(self.t), self.sems
            self.product(h, k)
            p, s, sp = prim[h], sec[h], self.order(h, k)
            ahead, behind = device(h, up1(p, 1), s), device(h, up1(p, 3), s)
            far, i = up1(p, 2), 2 * k
            remote(part.at[self.at(h, far, sp, "F")], relay_f.at[h, k, rows], sems, t, h, i + RELAY, ahead)
            remote(part.at[self.at(h, far, sp, "B")], relay_b.at[h, k, rows], sems, t, h, i + RELAY, behind)
            remote(part.at[self.at(h, up1(p, 1), sp, "B")], full_f.at[h, k, rows, QUART:], sems, t, h, i + FULL, ahead)
            remote(part.at[self.at(h, up1(p, 3), sp, "F")], full_b.at[h, k, rows, :QUART], sems, t, h, i + FULL, behind)

        def second(self, k):
            t, rows, sems = self.t, rows_of(self.t), self.sems
            for h in range(2):
                p, s, sp = prim[h], sec[h], self.order(h, k)
                ahead, behind = device(h, up1(p, 1), s), device(h, up1(p, 3), s)
                i = 2 * k
                wait_for(PIECE, rs_recv.at[t, h, i + RELAY])
                at = self.at(h, up1(p, 1), sp, "F")
                part[at] = (part[at].astype(F32) + relay_f[h, k, rows].astype(F32)).astype(BF16)
                remote(part.at[at], full_f.at[h, k, rows, :QUART], sems, t, h, i + FULL, ahead)
                at = self.at(h, up1(p, 3), sp, "B")
                part[at] = (part[at].astype(F32) + relay_b[h, k, rows].astype(F32)).astype(BF16)
                remote(part.at[at], full_b.at[h, k, rows, QUART:], sems, t, h, i + FULL, behind)

        def third(self, k):
            t, rows, sems = self.t, rows_of(self.t), self.sems
            for h in range(2):
                p, s, sp = prim[h], sec[h], self.order(h, k)
                wait_for(PAIR, rs_recv.at[t, h, 2 * k + FULL])
                value = (
                    part[self.at(h, p, sp, "W")].astype(F32)
                    + full_f[h, k, rows].astype(F32)
                    + full_b[h, k, rows].astype(F32)
                )
                ahead, behind = device(h, p, up1(s, 1)), device(h, p, up1(s, 3))
                if k == 0:
                    mid[h, 0, rows] = value.astype(BF16)
                    remote(mid.at[h, 0, rows, :QUART], relay2_f.at[h, rows], sems, t, h, R2F, ahead)
                    remote(mid.at[h, 0, rows, QUART:], relay2_b.at[h, rows], sems, t, h, R2B, behind)
                elif k == 1:
                    wait_for(UNIT, rs_recv.at[t, h, R2F])
                    mid[h, 1, rows, :QUART] = (value[:, :QUART] + relay2_f[h, rows].astype(F32)).astype(BF16)
                    mid[h, 1, rows, QUART:] = value[:, QUART:].astype(BF16)
                    remote(mid.at[h, 1, rows], full2_f.at[h, rows], sems, t, h, FULL2, ahead)
                elif k == 2:
                    wait_for(UNIT, rs_recv.at[t, h, R2B])
                    mid[h, 2, rows, :QUART] = value[:, :QUART].astype(BF16)
                    mid[h, 2, rows, QUART:] = (value[:, QUART:] + relay2_b[h, rows].astype(F32)).astype(BF16)
                    remote(mid.at[h, 2, rows], full2_b.at[h, rows], sems, t, h, FULL2, behind)
                else:
                    total[rows, cols_of(h, "W")] = value

        def last(self):
            rows = rows_of(self.t)
            for h in range(2):
                wait_for(PAIR, rs_recv.at[self.t, h, FULL2])
                wait_for(SENT, rs_send.at[self.t, h])
            return [
                total[rows, cols_of(h, "W")] + full2_f[h, rows].astype(F32) + full2_b[h, rows].astype(F32)
                for h in range(2)
            ]

    class Gather:
        def __init__(self, t):
            self.t = t
            self.sems = (ag_send, ag_recv)

        def order(self, h, k):
            return up1(sec[h], (0, 3, 1, 2)[k])

        def put(self, h, i, pp, sp, which, dev):
            a, b = place(h, pp, sp)
            ref = norm.at[a, b, rows_of(self.t), cols_of(h, which)]
            remote(ref, ref, self.sems, self.t, h, i, dev)

        def one(self, h, i, sp, which, by):
            self.put(h, i, prim[h], sp, which, device(h, prim[h], up1(sec[h], by)))

        def two(self, h, k, i, pp, which, by):
            self.put(h, 2 + 2 * k + i, pp, self.order(h, k), which, device(h, up1(prim[h], by), sec[h]))

        def own(self, h, k):
            self.two(h, k, OWN, prim[h], "W", 1)
            self.two(h, k, OWN, prim[h], "W", 3)

        def wait(self, h, i):
            wait_for(PAIR if i % 2 == OWN else PIECE, ag_recv.at[self.t, h, i])

        def norms(self, sums):
            rows = rows_of(self.t)
            for h in range(2):
                cs = cols_of(h, "W")
                resid[rows, cs] = hid[rows, cs].astype(F32) + sums[h]
            mean = jnp.sum(resid[rows], axis=1, keepdims=True) * (1.0 / WIDTH)
            centered = resid[rows] - mean
            var = jnp.sum(centered * centered, axis=1, keepdims=True) * (1.0 / WIDTH)
            norm[y, z, rows] = (centered * lax.rsqrt(var + EPS) * gain[...] + bias[...]).astype(BF16)

        def start(self):
            for h in range(2):
                self.one(h, OWN, sec[h], "W", 1)
                self.one(h, OWN, sec[h], "W", 3)
            for h in range(2):
                self.own(h, 0)

        def near(self):
            for h in range(2):
                self.wait(h, OWN)
                self.one(h, REL, up1(sec[h], 3), "F", 1)
                self.own(h, 1)
                self.one(h, REL, up1(sec[h], 1), "B", 3)
                self.own(h, 2)

        def far(self):
            for h in range(2):
                self.wait(h, REL)
                self.own(h, 3)

        def relay(self, k):
            for h in range(2):
                self.wait(h, 2 + 2 * k + OWN)
                self.two(h, k, REL, up1(prim[h], 3), "F", 1)
                self.two(h, k, REL, up1(prim[h], 1), "B", 3)

        def done(self, k):
            for h in range(2):
                self.wait(h, 2 + 2 * k + REL)

        def product(self, k, h):
            rows = rows_of(self.t)
            sp, cs = self.order(h, k), cols_of(h, "W")
            lhs = norm[:, sp, rows, cs] if h == 0 else norm[sp, :, rows, cs]
            value = nt_dot(lhs.reshape(64, HALF), wi[:, cs]).reshape(4, 16, UNITS)
            if h == 0:
                acc[:, sp, rows] = acc[:, sp, rows] + value
            else:
                acc[sp, :, rows] = acc[sp, :, rows] + value

        def low_copy(self, i):
            ref = low.at[self.t, m]
            return pltpu.make_async_remote_copy(
                src_ref=ref,
                dst_ref=ref,
                send_sem=low_send.at[self.t],
                recv_sem=low_recv.at[self.t],
                device_id={"mlp": lax.rem(m + i, 16)},
                device_id_type=MESH,
            )

        def inside(self, i):
            lane = lax.broadcasted_iota(jnp.int32, (RANK, 256), 1)
            token = (lane >> 4) * 32 + (lane & 15) + 16 * self.t
            return (token >= starts[i]) & (token < ends[i])

        def lows(self):
            window = pl.ds(pl.multiple_of(lax.div(m * 5 - lax.rem(m, 2), 2) * 128, 128), 384)
            ranks = nt_dot(dsel[...], norm[:, :, rows_of(self.t), window].reshape(256, 384))
            mine = jnp.zeros((RANK, 256), F32)
            for i in range(REQS):
                mine = mine + jnp.where(self.inside(i), ranks[i * RANK : (i + 1) * RANK, :], 0.0)
            low[self.t, m] = mine.astype(BF16)

            def low_start(i, c):
                self.low_copy(i).start()
                return c

            lax.fori_loop(1, 16, low_start, 0)

        def activate(self):
            t, rows = self.t, rows_of(self.t)
            wait_for(low.at[t, 0:15], low_recv.at[t])
            wait_for(low.at[t, 0:15], low_send.at[t])
            lowrank = jnp.sum(low[t].astype(F32), axis=0).astype(BF16).astype(F32)
            for i in range(REQS):
                spread[i * RANK : (i + 1) * RANK, :] = jnp.where(self.inside(i), lowrank, 0.0).astype(BF16)
            for i in range(2):
                adapted = lax.dot_general(
                    spread[:, i * 128 : (i + 1) * 128], usel[...], (((0,), (0,)), ((), ())), preferred_element_type=F32
                )
                two = slice(2 * i, 2 * i + 2)
                preact = acc[two, :, rows] + adapted.reshape(2, 4, 16, UNITS)
                act[two, :, rows] = jax.nn.gelu(preact, approximate=True).astype(BF16)
            for h in range(2):
                wait_for(SENT, ag_send.at[t, h])

    def pages():
        locals_[6].wait()
        locals_[7].wait()
        for t, cache, out in ((1, kc, ko), (2, vc, vo)):
            for page in range(5):
                value = cache[page]
                for b in range(4):
                    value = jnp.where(look[0, b] == page, qkv[t, b * 128 : (b + 1) * 128, :], value)
                out[page] = value

    def pick_down():
        for t, ref in enumerate((downs, ups)):
            wait_for(ref, fac_recv.at[t])
            wait_for(ref.at[0:7], fac_send.at[t])
        picked = jnp.dot(onehot[...], downs[...].reshape(64 * RANK, 320), preferred_element_type=F32)
        dsel_f[...] = jnp.zeros_like(dsel_f)
        dsel_f[:, :320] = picked
        shifted = jnp.where(lax.rem(m, 2) == 1, pltpu.roll(dsel_f[...], 64, 1), dsel_f[...])
        dsel[...] = shifted.astype(BF16)

    def pick_up():
        usel[...] = jnp.dot(onehot[...], ups[...].reshape(64 * RANK, UNITS), preferred_element_type=F32).astype(BF16)

    locals_[0].wait()
    locals_[3].wait()
    a, b = Scatter(0, att, wo), Scatter(1, att, wo)
    c, d = Scatter(0, act, w2), Scatter(1, act, w2)
    ga, gb = Gather(0), Gather(1)
    a.first(0, 0)
    a.first(0, 1)
    a.first(1, 0)
    a.first(1, 1)
    b.first(0, 0)
    b.first(0, 1)
    a.second(0)
    b.first(1, 0)
    b.first(1, 1)
    a.first(2, 0)
    a.first(2, 1)
    a.first(3, 0)
    a.first(3, 1)
    b.second(0)
    a.third(0)
    a.second(1)
    a.second(2)
    b.first(2, 0)
    b.first(2, 1)
    a.second(3)
    a.third(1)
    a.third(2)
    b.third(0)
    b.second(1)
    b.first(3, 0)
    b.first(3, 1)
    a.third(3)
    locals_[4].wait()
    locals_[5].wait()
    ga.norms(a.last())
    ga.start()
    b.second(2)
    ga.near()
    b.third(1)
    b.third(2)
    b.second(3)
    ga.far()
    ga.relay(2)
    ga.relay(0)
    pick_down()
    ga.relay(1)
    pick_up()
    b.third(3)
    ga.relay(3)
    gb.norms(b.last())
    gb.start()
    ga.done(2)
    pages()
    ga.done(0)
    locals_[1].wait()
    ga.product(2, 0)
    ga.product(2, 1)
    ga.done(3)
    ga.done(1)
    ga.lows()
    ga.product(3, 0)
    ga.product(3, 1)
    gb.near()
    ga.product(0, 0)
    ga.product(0, 1)
    gb.relay(0)
    ga.product(1, 0)
    ga.product(1, 1)
    ga.activate()
    gb.far()
    locals_[2].wait()
    c.first(0, 0)
    c.first(0, 1)
    gb.relay(1)
    gb.relay(2)
    gb.done(0)
    gb.product(0, 0)
    gb.product(0, 1)
    gb.relay(3)
    c.first(1, 0)
    c.first(1, 1)
    c.first(2, 0)
    c.first(2, 1)
    gb.done(1)
    c.second(0)
    gb.product(1, 0)
    gb.product(1, 1)
    gb.done(2)
    gb.done(3)
    gb.lows()
    c.second(1)
    c.first(3, 0)
    c.first(3, 1)
    gb.product(3, 0)
    gb.product(3, 1)
    gb.product(2, 0)
    gb.product(2, 1)
    c.third(0)
    c.second(2)
    c.second(3)
    gb.activate()
    d.first(0, 0)
    d.first(0, 1)
    d.first(1, 0)
    d.first(1, 1)
    d.first(2, 0)
    d.first(2, 1)
    d.second(0)
    d.second(1)
    d.first(3, 0)
    d.first(3, 1)
    d.third(0)
    d.second(2)
    d.second(3)
    c.third(1)
    c.third(2)
    d.third(1)
    c.third(3)
    d.third(2)
    sums = c.last()
    for h in range(2):
        outb[0:16, cols_of(h, "W")] = (resid[0:16, cols_of(h, "W")] + sums[h]).astype(BF16)
    d.third(3)
    sums = d.last()
    for h in range(2):
        outb[16:32, cols_of(h, "W")] = (resid[16:32, cols_of(h, "W")] + sums[h]).astype(BF16)
    wait_for(qkv.at[:, 0:480], a2a_send.at[0])


def writer(a, b, c, to_a, to_b, to_c, sem):
    copies = [pltpu.make_async_copy(x, o, sem.at[i]) for i, (x, o) in enumerate(((a, to_a), (b, to_b), (c, to_c)))]
    for copy in copies:
        copy.start()
    for copy in copies:
        copy.wait()


def written(results):
    any_ = pl.BlockSpec(memory_space=pl.ANY)
    return pl.pallas_call(
        writer,
        out_shape=tuple(jax.ShapeDtypeStruct(v.shape, v.dtype) for v in results),
        in_specs=[pl.BlockSpec(memory_space=pltpu.VMEM)] * 3,
        out_specs=(any_,) * 3,
        scratch_shapes=[pltpu.SemaphoreType.DMA((3,))],
    )(*(pltpu.with_memory_space_constraint(v, pltpu.VMEM) for v in results))


def shards(*args):
    (queries, keys, values, hidden, w_o, w_in, w_out, gain, bias, down, up, kc, vc, lens, look, adp, slot) = args
    any_, smem = pl.BlockSpec(memory_space=pl.ANY), pl.BlockSpec(memory_space=pltpu.SMEM)
    vmem, dma = pltpu.VMEM, pltpu.SemaphoreType.DMA
    scratch = [
        vmem((3, TOK_G, HEADC), BF16),
        vmem((4, 4, 32, HEADC), BF16),
        vmem((HEADC, WIDTH), BF16),
        vmem((UNITS, WIDTH), BF16),
        vmem((UNITS, WIDTH), BF16),
        vmem((32, WIDTH), BF16),
        vmem((1, WIDTH), F32),
        vmem((1, WIDTH), F32),
        vmem((8, 128, 320), BF16),
        vmem((8, 128, UNITS), BF16),
        vmem((5, 128, HEADC), BF16),
        vmem((5, 128, HEADC), BF16),
        vmem((TOK_G, 1), jnp.int32),
        vmem((4, 4, 32, WIDTH), BF16),
        vmem((4, 4, 32, WIDTH), BF16),
        vmem((2, 4, 32, QUART), BF16),
        vmem((2, 4, 32, QUART), BF16),
        vmem((2, 4, 32, HALF), BF16),
        vmem((2, 4, 32, HALF), BF16),
        vmem((2, 3, 32, HALF), BF16),
        vmem((2, 32, QUART), BF16),
        vmem((2, 32, QUART), BF16),
        vmem((2, 32, HALF), BF16),
        vmem((2, 32, HALF), BF16),
        vmem((32, WIDTH), F32),
        vmem((32, WIDTH), F32),
        vmem((4, 4, 32, UNITS), F32),
        vmem((4, 4, 32, UNITS), BF16),
        vmem((REQS * RANK, 64 * RANK), BF16),
        vmem((REQS * RANK, 384), F32),
        vmem((REQS * RANK, 384), BF16),
        vmem((REQS * RANK, UNITS), BF16),
        vmem((2, 16, RANK, 256), BF16),
        vmem((REQS * RANK, 256), BF16),
        dma((8,)),
        dma((1,)),
        dma((2,)),
        dma((2,)),
        dma((2,)),
        dma((2,)),
        dma((2,)),
        dma((2, 2)),
        dma((2, 2, 11)),
        dma((2, 2)),
        dma((2, 2, 10)),
    ]
    results = pl.pallas_call(
        kernel,
        out_shape=(
            pltpu.VMEM((32, WIDTH), BF16),
            pltpu.VMEM((5, 128, HEADC), BF16),
            pltpu.VMEM((5, 128, HEADC), BF16),
        ),
        in_specs=[any_] * 13 + [smem] * 4,
        out_specs=(pl.BlockSpec(memory_space=pltpu.VMEM),) * 3,
        scratch_shapes=scratch,
        compiler_params=pltpu.CompilerParams(
            collective_id=0, has_side_effects=True, vmem_limit_bytes=62 * 1024 * 1024
        ),
    )(
        queries, keys, values, hidden, w_o, w_in.T, w_out, gain.reshape(1, WIDTH), bias.reshape(1, WIDTH),
        jnp.transpose(down, (0, 2, 1)).reshape(128, 320), up.reshape(128, UNITS), kc, vc, lens, look, adp, slot,
    )
    return written(results)


def solution(mesh):
    in_specs = (
        P(("req", "mlp"), None),
        P(("req", "mlp"), None),
        P(("req", "mlp"), None),
        P(("req", "mlp"), None),
        P("mlp", None),
        P(None, "mlp"),
        P("mlp", None),
        P(),
        P(),
        P("req", "mlp", None),
        P("req", None, "mlp"),
        P("req", None, "mlp"),
        P("req", None, "mlp"),
        P("req", None),
        P("req", None),
        P("req", None),
        P(),
    )
    out_specs = (P(("req", "mlp"), None), P("req", None, "mlp"), P("req", None, "mlp"))
    return jax.shard_map(shards, mesh=mesh, in_specs=in_specs, out_specs=out_specs, check_vma=False)
```

```python
import functools

import jax
import jax.numpy as jnp
from jax import lax
from jax.experimental import pallas as pl
from jax.experimental.pallas import tpu as pltpu
from jax.sharding import PartitionSpec as P

MESH = pl.DeviceIdType.MESH
HS = 128
RANK = 16
REQS = 16
TOK_G = 512
WIDTH = 5120
HALF = WIDTH // 2
QUART = HALF // 2
UNITS = 864
HEADC = 256
TILE = 512
EPS = 1e-06
F32 = jnp.float32
BF16 = jnp.bfloat16

RELAY, FULL = range(2)
R2F, R2B, FULL2 = range(8, 11)
OWN, REL = range(2)


def nt_dot(a, b):
    return lax.dot_general(a, b, (((1,), (1,)), ((), ())), preferred_element_type=F32)


def kernel(
    q_hbm, k_hbm, v_hbm, hid_hbm, wo_hbm, wi_hbm, w2_hbm, gain_hbm, bias_hbm, down_hbm, up_hbm, kc_hbm, vc_hbm,
    lens, look, adp, slot,
    outb, ko, vo,
    qkv, att, wo, wi, w2, hid, gain, bias, downs, ups, kc, vc, start_col,
    part, norm, relay_f, relay_b, full_f, full_b, mid, relay2_f, relay2_b, full2_f, full2_b,
    resid, total, acc, act, onehot, dsel_f, dsel, usel, low, spread,
    local_sem, a2a_send, a2a_recv, fac_send, fac_recv, low_send, low_recv, rs_send, rs_recv, ag_send, ag_recv,
):
    m = lax.axis_index("mlp")
    r = lax.axis_index("req")
    y, z = lax.div(m, 4), lax.rem(m, 4)

    def place(h, p, s):
        return (p, s) if h == 0 else (s, p)

    def device(h, p, s):
        a, b = place(h, p, s)
        return {"mlp": a * 4 + b}

    prim = (y, z)
    sec = (z, y)

    def up1(i, by):
        return lax.rem(i + by, 4)

    def wait_for(like, sem):
        pltpu.make_async_copy(like, like, sem).wait()

    locals_ = {}

    def local(i, src, dst):
        c = pltpu.make_async_copy(src, dst, local_sem.at[i])
        c.start()
        locals_[i] = c

    local(0, wo_hbm, wo)
    local(3, hid_hbm, hid)
    local(4, gain_hbm, gain)
    local(5, bias_hbm, bias)
    local(6, kc_hbm, kc)
    local(7, vc_hbm, vc)
    pltpu.make_async_copy(down_hbm, downs.at[r], fac_recv.at[0]).start()
    pltpu.make_async_copy(up_hbm, ups.at[r], fac_recv.at[1]).start()
    own_rows = pl.ds(pl.multiple_of(m * 32, 32), 32)
    for h in range(2):
        for t, ref in enumerate((q_hbm, k_hbm, v_hbm)):
            cols = pl.ds(pl.multiple_of(m * HEADC + h * HS, HS), HS)
            mine = qkv.at[t, own_rows, h * HS : (h + 1) * HS]
            pltpu.make_async_copy(ref.at[:, cols], mine, a2a_recv.at[h]).start()

    barrier = pltpu.get_barrier_semaphore()

    def greet_mlp(i, c):
        pl.semaphore_signal(barrier, inc=1, device_id={"mlp": lax.rem(m + i, 16)}, device_id_type=MESH)
        return c

    def greet_req(i, c):
        pl.semaphore_signal(barrier, inc=1, device_id={"req": lax.rem(r + i, 8)}, device_id_type=MESH)
        return c

    lax.fori_loop(1, 16, greet_mlp, 0)
    lax.fori_loop(1, 8, greet_req, 0)
    pl.semaphore_wait(barrier, 22)

    def far_first(i):
        return lax.rem(2 + 3 * i + 3 * lax.div(i * (i - 1), 2), 4)

    def a2a_copy(h, t, ref, i):
        d = up1(y, far_first(lax.div(i, 4))) * 4 + up1(z, far_first(lax.rem(i, 4)))
        return pltpu.make_async_remote_copy(
            src_ref=ref.at[:, pl.ds(pl.multiple_of(d * HEADC + h * HS, HS), HS)],
            dst_ref=qkv.at[t, own_rows, h * HS : (h + 1) * HS],
            send_sem=a2a_send.at[0],
            recv_sem=a2a_recv.at[h],
            device_id={"mlp": d},
            device_id_type=MESH,
        )

    for h in range(2):

        def a2a_start(i, c, h=h):
            for t, ref in enumerate((q_hbm, k_hbm, v_hbm)):
                a2a_copy(h, t, ref, i).start()
            return c

        lax.fori_loop(0, 15, a2a_start, 0)

    def fac_copy(t, src, dst, i):
        return pltpu.make_async_remote_copy(
            src_ref=src,
            dst_ref=dst.at[r],
            send_sem=fac_send.at[t],
            recv_sem=fac_recv.at[t],
            device_id={"req": lax.rem(r + i, 8)},
            device_id_type=MESH,
        )

    def fac_start(i, c):
        fac_copy(0, down_hbm, downs, i).start()
        fac_copy(1, up_hbm, ups, i).start()
        return c

    lax.fori_loop(1, 8, fac_start, 0)
    local(1, wi_hbm, wi)
    local(2, w2_hbm, w2)

    pos = lax.broadcasted_iota(jnp.int32, (TOK_G, 1), 0)
    starts, ends = [], []
    first = jnp.zeros((TOK_G, 1), jnp.int32)
    end = jnp.int32(0)
    for i in range(REQS):
        starts.append(end)
        end = end + lens[0, i]
        ends.append(end)
        first = jnp.where(pos >= end, end, first)
    start_col[...] = first

    for i in range(REQS):
        wanted = slot[adp[0, i]] * RANK
        lane = lax.broadcasted_iota(jnp.int32, (RANK, 64 * RANK), 1)
        sub = lax.broadcasted_iota(jnp.int32, (RANK, 64 * RANK), 0)
        onehot[i * RANK : (i + 1) * RANK, :] = (lane - sub == wanted).astype(F32).astype(BF16)
    acc[...] = jnp.zeros_like(acc)


    for h in range(2):
        hc = slice(h * HS, (h + 1) * HS)
        wait_for(qkv.at[:, :, hc], a2a_recv.at[h])
        for i in range(4):
            rows, length = slice(i * 128, (i + 1) * 128), (i + 1) * 128
            score = nt_dot(qkv[0, rows, hc], qkv[1, :length, hc]) * (HS ** (-0.5))
            qi = lax.broadcasted_iota(jnp.int32, (128, length), 0) + i * 128
            kj = lax.broadcasted_iota(jnp.int32, (128, length), 1)
            allowed = (kj <= qi) & (kj >= start_col[rows, :])
            score = jnp.where(allowed, score, -1e30)
            expo = jnp.exp(score - jnp.max(score, axis=1, keepdims=True))
            weights = (expo / jnp.sum(expo, axis=1, keepdims=True)).astype(BF16)
            mixed = jnp.dot(weights, qkv[2, :length, hc], preferred_element_type=F32)
            att[i, :, :, hc] = mixed.astype(BF16).reshape(4, 32, HS)

    def remote(src, dst, sems, t, h, i, dev):
        c = pltpu.make_async_remote_copy(
            src_ref=src,
            dst_ref=dst,
            send_sem=sems[0].at[t, h],
            recv_sem=sems[1].at[t, h, i],
            device_id=dev,
            device_id_type=MESH,
        )
        c.start()

    def rows_of(t):
        return slice(16 * t, 16 * t + 16)

    def cols_of(h, which):
        base = h * HALF
        if which == "F":
            return slice(base, base + QUART)
        if which == "B":
            return slice(base + QUART, base + HALF)
        return slice(base, base + HALF)

    UNIT, PIECE, PAIR, SENT = wo.at[0:16, :QUART], wo.at[0:16, :HALF], wo.at[0:16], wo.at[0:240, :HALF]

    class Scatter:
        def __init__(self, t, left, right):
            self.t, self.left, self.right = t, left, right
            self.sems = (rs_send, rs_recv)

        def at(self, h, p, s, which):
            a, b = place(h, p, s)
            return (a, b, rows_of(self.t), cols_of(h, which))

        def order(self, h, k):
            return up1(sec[h], (2, 1, 3, 0)[k])

        def product(self, h, k):
            s, rows = self.order(h, k), rows_of(self.t)
            left, right = self.left, self.right
            lhs = left[:, s, rows] if h == 0 else left[s, :, rows]
            lhs = lhs.reshape(64, left.shape[3])
            for c in range(h * HALF, (h + 1) * HALF, TILE):
                value = jnp.dot(lhs, right[:, c : c + TILE], preferred_element_type=F32).astype(BF16)
                value = value.reshape(4, 16, TILE)
                if h == 0:
                    part[:, s, rows, c : c + TILE] = value
                else:
                    part[s, :, rows, c : c + TILE] = value

        def first(self, k, h):
            t, rows, sems = self.t, rows_of(self.t), self.sems
            self.product(h, k)
            p, s, sp = prim[h], sec[h], self.order(h, k)
            ahead, behind = device(h, up1(p, 1), s), device(h, up1(p, 3), s)
            far, i = up1(p, 2), 2 * k
            remote(part.at[self.at(h, far, sp, "F")], relay_f.at[h, k, rows], sems, t, h, i + RELAY, ahead)
            remote(part.at[self.at(h, far, sp, "B")], relay_b.at[h, k, rows], sems, t, h, i + RELAY, behind)
            remote(part.at[self.at(h, up1(p, 1), sp, "B")], full_f.at[h, k, rows, QUART:], sems, t, h, i + FULL, ahead)
            remote(part.at[self.at(h, up1(p, 3), sp, "F")], full_b.at[h, k, rows, :QUART], sems, t, h, i + FULL, behind)

        def second(self, k):
            t, rows, sems = self.t, rows_of(self.t), self.sems
            for h in range(2):
                p, s, sp = prim[h], sec[h], self.order(h, k)
                ahead, behind = device(h, up1(p, 1), s), device(h, up1(p, 3), s)
                i = 2 * k
                wait_for(PIECE, rs_recv.at[t, h, i + RELAY])
                at = self.at(h, up1(p, 1), sp, "F")
                part[at] = (part[at].astype(F32) + relay_f[h, k, rows].astype(F32)).astype(BF16)
                remote(part.at[at], full_f.at[h, k, rows, :QUART], sems, t, h, i + FULL, ahead)
                at = self.at(h, up1(p, 3), sp, "B")
                part[at] = (part[at].astype(F32) + relay_b[h, k, rows].astype(F32)).astype(BF16)
                remote(part.at[at], full_b.at[h, k, rows, QUART:], sems, t, h, i + FULL, behind)

        def third(self, k):
            t, rows, sems = self.t, rows_of(self.t), self.sems
            for h in range(2):
                p, s, sp = prim[h], sec[h], self.order(h, k)
                wait_for(PAIR, rs_recv.at[t, h, 2 * k + FULL])
                value = (
                    part[self.at(h, p, sp, "W")].astype(F32)
                    + full_f[h, k, rows].astype(F32)
                    + full_b[h, k, rows].astype(F32)
                )
                ahead, behind = device(h, p, up1(s, 1)), device(h, p, up1(s, 3))
                if k == 0:
                    mid[h, 0, rows] = value.astype(BF16)
                    remote(mid.at[h, 0, rows, :QUART], relay2_f.at[h, rows], sems, t, h, R2F, ahead)
                    remote(mid.at[h, 0, rows, QUART:], relay2_b.at[h, rows], sems, t, h, R2B, behind)
                elif k == 1:
                    wait_for(UNIT, rs_recv.at[t, h, R2F])
                    mid[h, 1, rows, :QUART] = (value[:, :QUART] + relay2_f[h, rows].astype(F32)).astype(BF16)
                    mid[h, 1, rows, QUART:] = value[:, QUART:].astype(BF16)
                    remote(mid.at[h, 1, rows], full2_f.at[h, rows], sems, t, h, FULL2, ahead)
                elif k == 2:
                    wait_for(UNIT, rs_recv.at[t, h, R2B])
                    mid[h, 2, rows, :QUART] = value[:, :QUART].astype(BF16)
                    mid[h, 2, rows, QUART:] = (value[:, QUART:] + relay2_b[h, rows].astype(F32)).astype(BF16)
                    remote(mid.at[h, 2, rows], full2_b.at[h, rows], sems, t, h, FULL2, behind)
                else:
                    total[rows, cols_of(h, "W")] = value

        def last(self):
            rows = rows_of(self.t)
            for h in range(2):
                wait_for(PAIR, rs_recv.at[self.t, h, FULL2])
                wait_for(SENT, rs_send.at[self.t, h])
            return [
                total[rows, cols_of(h, "W")] + full2_f[h, rows].astype(F32) + full2_b[h, rows].astype(F32)
                for h in range(2)
            ]

    class Gather:
        def __init__(self, t):
            self.t = t
            self.sems = (ag_send, ag_recv)

        def order(self, h, k):
            return up1(sec[h], (0, 3, 1, 2)[k])

        def put(self, h, i, pp, sp, which, dev):
            a, b = place(h, pp, sp)
            ref = norm.at[a, b, rows_of(self.t), cols_of(h, which)]
            remote(ref, ref, self.sems, self.t, h, i, dev)

        def one(self, h, i, sp, which, by):
            self.put(h, i, prim[h], sp, which, device(h, prim[h], up1(sec[h], by)))

        def two(self, h, k, i, pp, which, by):
            self.put(h, 2 + 2 * k + i, pp, self.order(h, k), which, device(h, up1(prim[h], by), sec[h]))

        def own(self, h, k):
            self.two(h, k, OWN, prim[h], "W", 1)
            self.two(h, k, OWN, prim[h], "W", 3)

        def wait(self, h, i):
            wait_for(PAIR if i % 2 == OWN else PIECE, ag_recv.at[self.t, h, i])

        def norms(self, sums):
            rows = rows_of(self.t)
            for h in range(2):
                cs = cols_of(h, "W")
                resid[rows, cs] = hid[rows, cs].astype(F32) + sums[h]
            mean = jnp.sum(resid[rows], axis=1, keepdims=True) * (1.0 / WIDTH)
            centered = resid[rows] - mean
            var = jnp.sum(centered * centered, axis=1, keepdims=True) * (1.0 / WIDTH)
            norm[y, z, rows] = (centered * lax.rsqrt(var + EPS) * gain[...] + bias[...]).astype(BF16)

        def start(self):
            for h in range(2):
                self.one(h, OWN, sec[h], "W", 1)
                self.one(h, OWN, sec[h], "W", 3)
            for h in range(2):
                self.own(h, 0)

        def near(self):
            for h in range(2):
                self.wait(h, OWN)
                self.one(h, REL, up1(sec[h], 3), "F", 1)
                self.own(h, 1)
                self.one(h, REL, up1(sec[h], 1), "B", 3)
                self.own(h, 2)

        def far(self):
            for h in range(2):
                self.wait(h, REL)
                self.own(h, 3)

        def relay(self, k):
            for h in range(2):
                self.wait(h, 2 + 2 * k + OWN)
                self.two(h, k, REL, up1(prim[h], 3), "F", 1)
                self.two(h, k, REL, up1(prim[h], 1), "B", 3)

        def done(self, k):
            for h in range(2):
                self.wait(h, 2 + 2 * k + REL)

        def product(self, k, h):
            rows = rows_of(self.t)
            sp, cs = self.order(h, k), cols_of(h, "W")
            lhs = norm[:, sp, rows, cs] if h == 0 else norm[sp, :, rows, cs]
            value = nt_dot(lhs.reshape(64, HALF), wi[:, cs]).reshape(4, 16, UNITS)
            if h == 0:
                acc[:, sp, rows] = acc[:, sp, rows] + value
            else:
                acc[sp, :, rows] = acc[sp, :, rows] + value

        def low_copy(self, i):
            ref = low.at[self.t, m]
            return pltpu.make_async_remote_copy(
                src_ref=ref,
                dst_ref=ref,
                send_sem=low_send.at[self.t],
                recv_sem=low_recv.at[self.t],
                device_id={"mlp": up1(y, far_first(lax.div(i, 4))) * 4 + up1(z, far_first(lax.rem(i, 4)))},
                device_id_type=MESH,
            )

        def inside(self, i):
            lane = lax.broadcasted_iota(jnp.int32, (RANK, 256), 1)
            token = (lane >> 4) * 32 + (lane & 15) + 16 * self.t
            return (token >= starts[i]) & (token < ends[i])

        def lows(self):
            window = pl.ds(pl.multiple_of(lax.div(m * 5 - lax.rem(m, 2), 2) * 128, 128), 384)
            ranks = nt_dot(dsel[...], norm[:, :, rows_of(self.t), window].reshape(256, 384))
            mine = jnp.zeros((RANK, 256), F32)
            for i in range(REQS):
                mine = mine + jnp.where(self.inside(i), ranks[i * RANK : (i + 1) * RANK, :], 0.0)
            low[self.t, m] = mine.astype(BF16)

            def low_start(i, c):
                self.low_copy(i).start()
                return c

            lax.fori_loop(0, 15, low_start, 0)

        def activate(self):
            t, rows = self.t, rows_of(self.t)
            wait_for(low.at[t, 0:15], low_recv.at[t])
            wait_for(low.at[t, 0:15], low_send.at[t])
            lowrank = jnp.sum(low[t].astype(F32), axis=0).astype(BF16).astype(F32)
            for i in range(REQS):
                spread[i * RANK : (i + 1) * RANK, :] = jnp.where(self.inside(i), lowrank, 0.0).astype(BF16)
            for i in range(2):
                adapted = lax.dot_general(
                    spread[:, i * 128 : (i + 1) * 128], usel[...], (((0,), (0,)), ((), ())), preferred_element_type=F32
                )
                two = slice(2 * i, 2 * i + 2)
                preact = acc[two, :, rows] + adapted.reshape(2, 4, 16, UNITS)
                act[two, :, rows] = jax.nn.gelu(preact, approximate=True).astype(BF16)
            for h in range(2):
                wait_for(SENT, ag_send.at[t, h])

    def pages():
        locals_[6].wait()
        locals_[7].wait()
        for t, cache, out in ((1, kc, ko), (2, vc, vo)):
            for page in range(5):
                value = cache[page]
                for b in range(4):
                    value = jnp.where(look[0, b] == page, qkv[t, b * 128 : (b + 1) * 128, :], value)
                out[page] = value

    def pick_down():
        for t, ref in enumerate((downs, ups)):
            wait_for(ref, fac_recv.at[t])
            wait_for(ref.at[0:7], fac_send.at[t])
        picked = jnp.dot(onehot[...], downs[...].reshape(64 * RANK, 320), preferred_element_type=F32)
        dsel_f[...] = jnp.zeros_like(dsel_f)
        dsel_f[:, :320] = picked
        shifted = jnp.where(lax.rem(m, 2) == 1, pltpu.roll(dsel_f[...], 64, 1), dsel_f[...])
        dsel[...] = shifted.astype(BF16)

    def pick_up():
        usel[...] = jnp.dot(onehot[...], ups[...].reshape(64 * RANK, UNITS), preferred_element_type=F32).astype(BF16)

    locals_[0].wait()
    locals_[3].wait()
    a, b = Scatter(0, att, wo), Scatter(1, att, wo)
    c, d = Scatter(0, act, w2), Scatter(1, act, w2)
    ga, gb = Gather(0), Gather(1)
    a.first(0, 0)
    a.first(0, 1)
    a.first(1, 0)
    a.first(1, 1)
    b.first(0, 0)
    b.first(0, 1)
    a.second(0)
    b.first(1, 0)
    b.first(1, 1)
    a.first(2, 0)
    a.first(2, 1)
    a.first(3, 0)
    a.first(3, 1)
    b.second(0)
    a.third(0)
    a.second(1)
    a.second(2)
    b.first(2, 0)
    b.first(2, 1)
    a.second(3)
    a.third(1)
    a.third(2)
    b.third(0)
    b.second(1)
    b.first(3, 0)
    b.first(3, 1)
    a.third(3)
    locals_[4].wait()
    locals_[5].wait()
    ga.norms(a.last())
    ga.start()
    b.second(2)
    ga.near()
    b.third(1)
    b.third(2)
    b.second(3)
    ga.far()
    ga.relay(2)
    ga.relay(0)
    pick_down()
    ga.relay(1)
    pick_up()
    b.third(3)
    ga.relay(3)
    gb.norms(b.last())
    gb.start()
    ga.done(2)
    pages()
    ga.done(0)
    locals_[1].wait()
    ga.product(2, 0)
    ga.product(2, 1)
    ga.done(3)
    ga.done(1)
    ga.lows()
    ga.product(3, 0)
    ga.product(3, 1)
    gb.near()
    ga.product(0, 0)
    ga.product(0, 1)
    gb.relay(0)
    ga.product(1, 0)
    ga.product(1, 1)
    ga.activate()
    gb.far()
    locals_[2].wait()
    c.first(0, 0)
    c.first(0, 1)
    gb.relay(1)
    gb.relay(2)
    gb.done(0)
    gb.product(0, 0)
    gb.product(0, 1)
    gb.relay(3)
    c.first(1, 0)
    c.first(1, 1)
    c.first(2, 0)
    c.first(2, 1)
    gb.done(1)
    c.second(0)
    gb.product(1, 0)
    gb.product(1, 1)
    gb.done(2)
    gb.done(3)
    gb.lows()
    c.second(1)
    c.first(3, 0)
    c.first(3, 1)
    gb.product(3, 0)
    gb.product(3, 1)
    gb.product(2, 0)
    gb.product(2, 1)
    c.third(0)
    c.second(2)
    c.second(3)
    gb.activate()
    d.first(0, 0)
    d.first(0, 1)
    d.first(1, 0)
    d.first(1, 1)
    d.first(2, 0)
    d.first(2, 1)
    d.second(0)
    d.second(1)
    d.first(3, 0)
    d.first(3, 1)
    d.third(0)
    d.second(2)
    d.second(3)
    c.third(1)
    c.third(2)
    d.third(1)
    c.third(3)
    d.third(2)
    sums = c.last()
    for h in range(2):
        outb[0:16, cols_of(h, "W")] = (resid[0:16, cols_of(h, "W")] + sums[h]).astype(BF16)
    d.third(3)
    sums = d.last()
    for h in range(2):
        outb[16:32, cols_of(h, "W")] = (resid[16:32, cols_of(h, "W")] + sums[h]).astype(BF16)
    wait_for(qkv.at[:, 0:480], a2a_send.at[0])


def writer(a, b, c, to_a, to_b, to_c, sem):
    copies = [pltpu.make_async_copy(x, o, sem.at[i]) for i, (x, o) in enumerate(((a, to_a), (b, to_b), (c, to_c)))]
    for copy in copies:
        copy.start()
    for copy in copies:
        copy.wait()


def written(results):
    any_ = pl.BlockSpec(memory_space=pl.ANY)
    return pl.pallas_call(
        writer,
        out_shape=tuple(jax.ShapeDtypeStruct(v.shape, v.dtype) for v in results),
        in_specs=[pl.BlockSpec(memory_space=pltpu.VMEM)] * 3,
        out_specs=(any_,) * 3,
        scratch_shapes=[pltpu.SemaphoreType.DMA((3,))],
    )(*(pltpu.with_memory_space_constraint(v, pltpu.VMEM) for v in results))


def shards(*args):
    (queries, keys, values, hidden, w_o, w_in, w_out, gain, bias, down, up, kc, vc, lens, look, adp, slot) = args
    any_, smem = pl.BlockSpec(memory_space=pl.ANY), pl.BlockSpec(memory_space=pltpu.SMEM)
    vmem, dma = pltpu.VMEM, pltpu.SemaphoreType.DMA
    scratch = [
        vmem((3, TOK_G, HEADC), BF16),
        vmem((4, 4, 32, HEADC), BF16),
        vmem((HEADC, WIDTH), BF16),
        vmem((UNITS, WIDTH), BF16),
        vmem((UNITS, WIDTH), BF16),
        vmem((32, WIDTH), BF16),
        vmem((1, WIDTH), F32),
        vmem((1, WIDTH), F32),
        vmem((8, 128, 320), BF16),
        vmem((8, 128, UNITS), BF16),
        vmem((5, 128, HEADC), BF16),
        vmem((5, 128, HEADC), BF16),
        vmem((TOK_G, 1), jnp.int32),
        vmem((4, 4, 32, WIDTH), BF16),
        vmem((4, 4, 32, WIDTH), BF16),
        vmem((2, 4, 32, QUART), BF16),
        vmem((2, 4, 32, QUART), BF16),
        vmem((2, 4, 32, HALF), BF16),
        vmem((2, 4, 32, HALF), BF16),
        vmem((2, 3, 32, HALF), BF16),
        vmem((2, 32, QUART), BF16),
        vmem((2, 32, QUART), BF16),
        vmem((2, 32, HALF), BF16),
        vmem((2, 32, HALF), BF16),
        vmem((32, WIDTH), F32),
        vmem((32, WIDTH), F32),
        vmem((4, 4, 32, UNITS), F32),
        vmem((4, 4, 32, UNITS), BF16),
        vmem((REQS * RANK, 64 * RANK), BF16),
        vmem((REQS * RANK, 384), F32),
        vmem((REQS * RANK, 384), BF16),
        vmem((REQS * RANK, UNITS), BF16),
        vmem((2, 16, RANK, 256), BF16),
        vmem((REQS * RANK, 256), BF16),
        dma((8,)),
        dma((1,)),
        dma((2,)),
        dma((2,)),
        dma((2,)),
        dma((2,)),
        dma((2,)),
        dma((2, 2)),
        dma((2, 2, 11)),
        dma((2, 2)),
        dma((2, 2, 10)),
    ]
    results = pl.pallas_call(
        kernel,
        out_shape=(
            pltpu.VMEM((32, WIDTH), BF16),
            pltpu.VMEM((5, 128, HEADC), BF16),
            pltpu.VMEM((5, 128, HEADC), BF16),
        ),
        in_specs=[any_] * 13 + [smem] * 4,
        out_specs=(pl.BlockSpec(memory_space=pltpu.VMEM),) * 3,
        scratch_shapes=scratch,
        compiler_params=pltpu.CompilerParams(
            collective_id=0, has_side_effects=True, vmem_limit_bytes=62 * 1024 * 1024
        ),
    )(
        queries, keys, values, hidden, w_o, w_in.T, w_out, gain.reshape(1, WIDTH), bias.reshape(1, WIDTH),
        jnp.transpose(down, (0, 2, 1)).reshape(128, 320), up.reshape(128, UNITS), kc, vc, lens, look, adp, slot,
    )
    return written(results)


def solution(mesh):
    in_specs = (
        P(("req", "mlp"), None),
        P(("req", "mlp"), None),
        P(("req", "mlp"), None),
        P(("req", "mlp"), None),
        P("mlp", None),
        P(None, "mlp"),
        P("mlp", None),
        P(),
        P(),
        P("req", "mlp", None),
        P("req", None, "mlp"),
        P("req", None, "mlp"),
        P("req", None, "mlp"),
        P("req", None),
        P("req", None),
        P("req", None),
        P(),
    )
    out_specs = (P(("req", "mlp"), None), P("req", None, "mlp"), P("req", None, "mlp"))
    return jax.shard_map(shards, mesh=mesh, in_specs=in_specs, out_specs=out_specs, check_vma=False)
```
